32 devices in a mesh: dp: 16 (over z, x, core), tensor: 2 (over y).
Axes of the slice: x: 2, y: 2, z: 4, core: 2. Of those that a mesh axis runs over, the one named last changes fastest.
Arguments:
- tokens: bfloat16 [32768, 768], P('dp'), may hold values from -6 to 6
- lengths: int32 [64], P('dp'), may hold values from 64 to 512, as said below
- w_qkv: bfloat16 [768, 3, 768], P(None, None, 'tensor'), may hold values from -0.21875 to 0.21875
- q_bias: float32 [768], P('tensor'), may hold values from -3 to 3
- v_bias: float32 [768], P('tensor'), may hold values from -3 to 3
- w_out: bfloat16 [768, 768], P('tensor'), may hold values from -0.875 to 0.875
- out_bias: float32 [768], replicated, may hold values from -2 to 2
- gain_one: float32 [768], replicated, may hold values from 0.5 to 1.5
- shift_one: float32 [768], replicated, may hold values from -2 to 2
- w_in: bfloat16 [768, 3072], P(None, 'tensor'), may hold values from -0.21875 to 0.21875
- in_bias: float32 [3072], P('tensor'), may hold values from -3 to 3
- w_down: bfloat16 [3072, 768], P('tensor'), may hold values from -0.15625 to 0.15625
- down_bias: float32 [768], replicated, may hold values from -2 to 2
- gain_two: float32 [768], replicated, may hold values from 0.5 to 1.5
- shift_two: float32 [768], replicated, may hold values from -2 to 2
- cotangent: bfloat16 [32768, 768], P(('dp', 'tensor')), may hold values from -6 to 6
Outputs:
- output: bfloat16 [32768, 768], P(('dp', 'tensor'))
- input_grad: bfloat16 [32768, 768], P(('dp', 'tensor'))
- grad_w_qkv: float32 [768, 3, 768], P(None, None, 'tensor')
- grad_q_bias: float32 [768], P('tensor')
- grad_v_bias: float32 [768], P('tensor')
- grad_w_out: float32 [768, 768], P('tensor')
- grad_out_bias: float32 [768], replicated
- grad_gain_one: float32 [768], replicated
- grad_shift_one: float32 [768], replicated
- grad_w_in: float32 [768, 3072], P(None, 'tensor')
- grad_in_bias: float32 [3072], P('tensor')
- grad_w_down: float32 [3072, 768], P('tensor')
- grad_down_bias: float32 [768], replicated
- grad_gain_two: float32 [768], replicated
- grad_shift_two: float32 [768], replicated
The draws below stay inside these ranges and needn't reach their ends.
Inputs may be any that keep to these rules, and one draw needn't show every extreme that they name: `lengths`: each sequence's valid tokens are its first ones; at least one sequence has all 512 tokens valid.
All inputs are finite; a program needn't handle non-finite values.
Results may differ from the reference program's by a relative error of at most 0.015.
Values may be sent and summed in bfloat16 or wider, within the bound.
No kernel may reach another device: no remote copies, remote signals or barrier semaphores. Data moves between devices by JAX's collectives and lax.ppermute only.
A program may use at most 192 MiB of HBM per device.

```python
import jax
import jax.numpy as jnp
from jax import lax

D = 768
HEADS = 12
HEAD_DIM = 64
FF = 3072
SEQ = 512
SEQS = 64
TOKENS = 32768


def draw_lengths(key, part):
    drawn = jax.random.randint(key, (SEQS,), SEQ // 8, SEQ + 1, dtype=jnp.int32)
    return drawn.at[0].set(SEQ)


def levels(stream_key, shape, split, smallest, high):
    def one(dim, blocks):
        steps = jax.random.uniform(jax.random.fold_in(jax.random.fold_in(stream_key, 6), dim), (blocks,), jnp.float32, smallest / len(split), high / len(split))
        return jnp.repeat(jnp.exp(steps), shape[dim] // blocks).reshape((-1,) + (1,) * (len(shape) - dim - 1))

    level = one(*split[0])
    for cut in split[1:]:
        level = level * one(*cut)
    return level


def scatter_about(stream_key, extent, width, limit, split=(), held_as=jnp.bfloat16):
    values = width * jax.random.normal(stream_key, extent, jnp.float32)
    if split:
        values = values * levels(stream_key, extent, split, -0.22, 0.18)
    return jnp.clip(values, -limit, limit).astype(held_as)


def setup_inputs(seed: int = 0) -> dict:
    splits = jax.random.split(jax.random.key(seed), 17)
    tokens = scatter_about(splits[0], (TOKENS, D), 1.0, 6.0, ((0, 16),))
    lengths = draw_lengths(jax.random.fold_in(splits[16], 71), 0)
    w_qkv = scatter_about(splits[2], (D, 3, D), D ** -0.5, 0.21875, ((2, 2),))
    q_bias = scatter_about(splits[3], (D,), 0.5, 3.0, ((0, 2),), jnp.float32)
    v_bias = scatter_about(splits[4], (D,), 0.5, 3.0, ((0, 2),), jnp.float32)
    w_out = scatter_about(splits[5], (D, D), (D // 16) ** -0.5, 0.875, ((0, 2),))
    out_bias = scatter_about(splits[6], (D,), 0.3, 2.0, (), jnp.float32)
    gain_one = jnp.clip(1.0 + 0.1 * jax.random.normal(splits[7], (D,), jnp.float32), 0.5, 1.5)
    shift_one = scatter_about(splits[8], (D,), 0.3, 2.0, (), jnp.float32)
    w_in = scatter_about(splits[9], (D, FF), D ** -0.5, 0.21875, ((1, 2),))
    in_bias = scatter_about(splits[10], (FF,), 0.5, 3.0, ((0, 2),), jnp.float32)
    w_down = scatter_about(splits[11], (FF, D), (FF // 2) ** -0.5, 0.15625, ((0, 2),))
    down_bias = scatter_about(splits[12], (D,), 0.3, 2.0, (), jnp.float32)
    gain_two = jnp.clip(1.0 + 0.1 * jax.random.normal(splits[13], (D,), jnp.float32), 0.5, 1.5)
    shift_two = scatter_about(splits[14], (D,), 0.3, 2.0, (), jnp.float32)
    cotangent = scatter_about(splits[15], (TOKENS, D), 1.0, 6.0, ((0, 32),))
    return {"tokens": tokens, "lengths": lengths, "w_qkv": w_qkv, "q_bias": q_bias, "v_bias": v_bias, "w_out": w_out, "out_bias": out_bias, "gain_one": gain_one, "shift_one": shift_one, "w_in": w_in, "in_bias": in_bias, "w_down": w_down, "down_bias": down_bias, "gain_two": gain_two, "shift_two": shift_two, "cotangent": cotangent}


@jax.custom_vjp
def low(v):
    return lax.optimization_barrier(v.astype(jnp.bfloat16)).astype(jnp.float32)

@jax.custom_vjp
def low_back(v):
    return v

def low_keep(v):
    return (low(v), None)

def low_pass(kept, grad):
    return (grad,)

def back_keep(v):
    return (v, None)

def back_low(kept, grad):
    return (low(grad),)
low.defvjp(low_keep, low_pass)
low_back.defvjp(back_keep, back_low)
EPSILON = 1e-06
MASKED = -1000000000.0
HIGHEST_PREC = lax.Precision.HIGHEST

def layer_norm(values, norm_gain, norm_shift):
    average = lax.optimization_barrier(jnp.mean(values, axis=-1, keepdims=True))
    centred = values - average
    variance = lax.optimization_barrier(jnp.mean(centred * centred, axis=-1, keepdims=True))
    return centred * lax.rsqrt(variance + EPSILON) * norm_gain + norm_shift

def forward(inputs, seq_lengths, w_qkv, q_bias, v_bias, w_out, out_bias, gain_one, shift_one, w_in, in_bias, w_down, down_bias, gain_two, shift_two):
    seq_count = seq_lengths.shape[0]
    rounded = low(inputs)
    project = jnp.einsum('td,dcf->tcf', rounded, w_qkv, precision=HIGHEST_PREC)
    queries = low_back(low(project[:, 0] + q_bias)).reshape(seq_count, SEQ, HEADS, HEAD_DIM)
    key_rows = low_back(low(project[:, 1])).reshape(seq_count, SEQ, HEADS, HEAD_DIM)
    values = low_back(low(project[:, 2] + v_bias)).reshape(seq_count, SEQ, HEADS, HEAD_DIM)
    scores = jnp.einsum('sqhe,skhe->shqk', queries, key_rows, precision=HIGHEST_PREC) * HEAD_DIM ** (-0.5)
    scores = low_back(scores)
    valid = lax.iota(jnp.int32, SEQ)[None, :] < seq_lengths[:, None]
    scores = jnp.where(valid[:, None, None, :], scores, MASKED)
    attn_probs = jax.nn.softmax(scores, axis=-1)
    context = jnp.einsum('shqk,skhe->sqhe', low(attn_probs), values, precision=HIGHEST_PREC)
    context = low_back(low(context.reshape(seq_count * SEQ, D)))
    attended = low_back(jnp.dot(context, w_out, precision=HIGHEST_PREC))
    hidden_one = layer_norm(attended + out_bias + inputs, gain_one, shift_one)
    pre_act = low_back(jnp.dot(low(hidden_one), w_in, precision=HIGHEST_PREC) + in_bias)
    activated = low(jax.nn.gelu(pre_act, approximate=False))
    branch = low_back(jnp.dot(activated, w_down, precision=HIGHEST_PREC))
    return layer_norm(branch + down_bias + hidden_one, gain_two, shift_two)

def reference(tokens, lengths, w_qkv, q_bias, v_bias, w_out, out_bias, gain_one, shift_one, w_in, in_bias, w_down, down_bias, gain_two, shift_two, cotangent):
    weights_all = tuple((weight.astype(jnp.float32) for weight in (w_qkv, q_bias, v_bias, w_out, out_bias, gain_one, shift_one, w_in, in_bias, w_down, down_bias, gain_two, shift_two)))
    groups = tokens.shape[0] // (8 * SEQ)
    tok_blocks = tokens.astype(jnp.float32).reshape(groups, 8 * SEQ, D)
    len_blocks = lengths.reshape(groups, 8)
    cot_blocks = cotangent.astype(jnp.float32).reshape(groups, 8 * SEQ, D)

    def one_group(totals, entries):
        inputs, seq_lengths, cot_rows = entries

        def run(inputs, *weights):
            return forward(inputs, seq_lengths, *weights)
        result, pullback = jax.vjp(run, inputs, *weights_all)
        grads = pullback(cot_rows)
        totals = tuple((total + grad for total, grad in zip(totals, grads[1:])))
        return (totals, (result, grads[0]))
    zeros = tuple((jnp.zeros_like(weight) for weight in weights_all))
    totals, (results, input_grads) = lax.scan(one_group, zeros, (tok_blocks, len_blocks, cot_blocks))
    output = results.reshape(tokens.shape[0], D).astype(jnp.bfloat16)
    input_grad = input_grads.reshape(tokens.shape[0], D).astype(jnp.bfloat16)
    return (output, input_grad, totals[0], totals[1], totals[2], totals[3], totals[4], totals[5], totals[6], totals[7], totals[8], totals[9], totals[10], totals[11], totals[12])
```

```python
import jax
import jax.numpy as jnp
from jax import lax
from jax.experimental import pallas as pl
from jax.experimental.pallas import tpu as pltpu
from jax.sharding import PartitionSpec as P

HEAD_DIM = 64
EPSILON = 1e-06
MASKED = -1000000000.0
LOW = jnp.bfloat16
WIDE = jnp.float32
RSQRT2 = 0.7071067811865476
RSQRT2PI = 0.3989422804014327


def contract(a, b, dim_a, dim_b):
    return lax.dot_general(
        a, b, (((dim_a,), (dim_b,)), ((), ())), preferred_element_type=WIDE
    )


def halves(d):
    return d & 1, (d >> 1) & 1, (d >> 2) & 1


def swap(array, bit, size):
    return lax.ppermute(array, "dp", [(i, i ^ (1 << bit)) for i in range(size)])


def across(array):
    return lax.ppermute(array, "tensor", [(0, 1), (1, 0)])


def attend_kernel(length_ref, q_ref, k_ref, v_ref, context_ref, probs_ref):
    length = length_ref[pl.program_id(0)]
    rows = q_ref.shape[0]
    lane = lax.broadcasted_iota(jnp.int32, (rows, 128), 1)
    slot = lax.broadcasted_iota(jnp.int32, (rows, 128), 0)
    masked = jnp.where(slot < length, 0.0, MASKED).astype(LOW)
    q, k, v = q_ref[...], k_ref[...], v_ref[...]
    zero, one = jnp.zeros_like(q), jnp.ones_like(q)
    contexts = []
    for head in range(2):
        mine = (lane >= 64) if head else (lane < 64)
        mark = lane == (0 if head else 64)
        k_head = jnp.where(mine, k, jnp.where(mark, masked, zero))
        q_head = jnp.where(mine, q, jnp.where(mark, one, zero))
        scores = contract(k_head, q_head, 1, 1)
        top = jnp.max(scores, axis=0, keepdims=True)
        exponent = jnp.exp(scores - top)
        total = jnp.sum(exponent, axis=0, keepdims=True)
        probs = (exponent * (1.0 / total)).astype(LOW)
        probs_ref[head] = probs
        contexts.append(contract(probs, v, 0, 0))
    context_ref[...] = jnp.where(lane < 64, contexts[0], contexts[1]).astype(LOW)


def attend(lengths, q, k, v):
    rows, width = q.shape
    sequences = lengths.shape[0]
    length, pairs = rows // sequences, width // 128
    block = pl.BlockSpec((length, 128), lambda s, h, *_: (s, h))
    return pl.pallas_call(
        attend_kernel,
        grid_spec=pltpu.PrefetchScalarGridSpec(
            num_scalar_prefetch=1,
            grid=(sequences, pairs),
            in_specs=[block] * 3,
            out_specs=[
                block,
                pl.BlockSpec((2, length, length), lambda s, h, *_: (s * pairs + h, 0, 0)),
            ],
        ),
        out_shape=[
            jax.ShapeDtypeStruct((rows, width), LOW),
            jax.ShapeDtypeStruct((sequences * pairs * 2, length, length), LOW),
        ],
        cost_estimate=pl.CostEstimate(
            flops=11 * 10**9, bytes_accessed=10**7, transcendentals=10**6
        ),
        name="attend",
    )(lengths, q, k, v)


def attend_back_kernel(q_ref, k_ref, v_ref, context_ref, grad_ref, probs_ref, out_ref):
    rows = q_ref.shape[0]
    lane = lax.broadcasted_iota(jnp.int32, (rows, 128), 1)
    q, k, v, grad = q_ref[...], k_ref[...], v_ref[...], grad_ref[...]
    inner = pltpu.roll(grad.astype(WIDE) * context_ref[...].astype(WIDE), 64, 1).astype(LOW)
    zero, minus = jnp.zeros_like(q), -jnp.ones_like(q)
    grad_q = grad_k = grad_v = 0.0
    for head in range(2):
        mine = (lane >= 64) if head else (lane < 64)
        centred = contract(jnp.where(mine, v, minus), jnp.where(mine, grad, inner), 1, 1)
        probs = probs_ref[head]
        grad_scores = (probs.astype(WIDE) * centred).astype(LOW)
        grad_v += contract(probs, jnp.where(mine, grad, zero), 1, 0)
        grad_k += contract(grad_scores, jnp.where(mine, q, zero), 1, 0)
        grad_q += contract(grad_scores, jnp.where(mine, k, zero), 0, 0)
    out_ref[0] = (grad_q * HEAD_DIM**-0.5).astype(LOW)
    out_ref[1] = grad_k.astype(LOW)
    out_ref[2] = grad_v.astype(LOW)


def attend_back(q, k, v, context, grad, probs, sequences):
    rows, width = q.shape
    length, pairs = rows // sequences, width // 128
    block = pl.BlockSpec((length, 128), lambda s, h: (s, h))
    return pl.pallas_call(
        attend_back_kernel,
        grid=(sequences, pairs),
        in_specs=[block] * 5
        + [pl.BlockSpec((2, length, length), lambda s, h: (s * pairs + h, 0, 0))],
        out_specs=pl.BlockSpec((3, length, 128), lambda s, h: (0, s, h)),
        out_shape=jax.ShapeDtypeStruct((3, rows, width), LOW),
        cost_estimate=pl.CostEstimate(
            flops=12 * 10**9, bytes_accessed=10**7, transcendentals=0
        ),
        name="attend_back",
    )(q, k, v, context, grad, probs)


def down_kernel(bits_ref, a_ref, b_ref, *refs):
    out_ref = refs[-1]
    z = bits_ref[2]
    result = contract(a_ref[...], b_ref[...], 0, 0)
    rows = result.shape[0] // 2
    for part in range(2):
        piece = result[part * rows : (part + 1) * rows]
        if len(refs) == 2:
            piece = piece + refs[0][0, part ^ z].astype(WIDE)
        out_ref[0, part ^ z] = piece.astype(LOW)


def down_pieces(bits, send, activated, grad, *received):
    rows, hidden = activated.shape
    width = grad.shape[1]
    block = pl.BlockSpec((1, 2, hidden // 8, width), lambda i, s: (i, 0, 0, 0))
    return pl.pallas_call(
        down_kernel,
        grid_spec=pltpu.PrefetchScalarGridSpec(
            num_scalar_prefetch=1,
            grid=(2,),
            in_specs=[
                pl.BlockSpec((rows, hidden // 4), lambda i, s: (0, (s[0] ^ send) * 2 + (i ^ s[1]))),
                pl.BlockSpec((rows, width), lambda i, s: (0, 0)),
            ]
            + [block] * len(received),
            out_specs=block,
        ),
        out_shape=jax.ShapeDtypeStruct((2, 2, hidden // 8, width), LOW),
        cost_estimate=pl.CostEstimate(flops=3 * 10**9, bytes_accessed=10**6, transcendentals=0),
        name="down_pieces",
    )(bits, activated, grad, *received)


def up_pieces(bits, send, hidden_rows, grad, *received):
    rows, width = hidden_rows.shape
    hidden = grad.shape[1]
    block = pl.BlockSpec((1, 2, width // 2, hidden // 4), lambda i, s: (i, 0, 0, 0))
    return pl.pallas_call(
        down_kernel,
        grid_spec=pltpu.PrefetchScalarGridSpec(
            num_scalar_prefetch=1,
            grid=(2,),
            in_specs=[
                pl.BlockSpec((rows, width), lambda i, s: (0, 0)),
                pl.BlockSpec((rows, hidden // 4), lambda i, s: (0, (s[0] ^ send) * 2 + (i ^ s[1]))),
            ]
            + [block] * len(received),
            out_specs=block,
        ),
        out_shape=jax.ShapeDtypeStruct((2, 2, width // 2, hidden // 4), LOW),
        cost_estimate=pl.CostEstimate(flops=3 * 10**9, bytes_accessed=10**6, transcendentals=0),
        name="up_pieces",
    )(bits, hidden_rows, grad, *received)


def heads_kernel(bits_ref, x_ref, g_ref, context_ref, grad_ref, *refs):
    out_ref = refs[-1]
    mine = bits_ref[1] * 2 + bits_ref[2]

    def put(result):
        rows = result.shape[0] // 4
        for part in range(4):
            piece = result[part * rows : (part + 1) * rows]
            if len(refs) == 2:
                piece = piece + refs[0][part ^ mine, 0].astype(WIDE)
            out_ref[part ^ mine, 0] = piece.astype(LOW)

    @pl.when(pl.program_id(0) < 3)
    def _():
        put(contract(x_ref[...], g_ref[0], 0, 0))

    @pl.when(pl.program_id(0) == 3)
    def _():
        put(contract(context_ref[...], grad_ref[...], 0, 0))


def heads_pieces(bits, send, tokens, grads, context, grad, *received):
    rows, width = tokens.shape
    local = context.shape[1]
    block = pl.BlockSpec((4, 1, width // 8, local), lambda j, s: (0, j, 0, 0))
    return pl.pallas_call(
        heads_kernel,
        grid_spec=pltpu.PrefetchScalarGridSpec(
            num_scalar_prefetch=1,
            grid=(4,),
            in_specs=[
                pl.BlockSpec((rows, width // 2), lambda j, s: (0, s[0] ^ send)),
                pl.BlockSpec((1, rows, local), lambda j, s: (jnp.minimum(j, 2), 0, 0)),
                pl.BlockSpec((rows, local), lambda j, s: (0, 0)),
                pl.BlockSpec((rows, width // 2), lambda j, s: (0, s[0] ^ send)),
            ]
            + [block] * len(received),
            out_specs=block,
        ),
        out_shape=jax.ShapeDtypeStruct((4, 4, width // 8, local), LOW),
        cost_estimate=pl.CostEstimate(flops=3 * 10**9, bytes_accessed=10**6, transcendentals=0),
        name="heads_pieces",
    )(bits, tokens, grads, context, grad, *received)


def add(*arrays):
    total = arrays[0].astype(WIDE)
    for array in arrays[1:]:
        total = total + array.astype(WIDE)
    return total.astype(LOW)


def sum_pieces(own, other, size):
    arrived = across(other)
    here = swap(add(own[1], arrived[1]), 1, size)
    kept = add(own[0], arrived[0], here)
    kept = add(kept[0], swap(kept[1], 2, size))
    for bit in range(3, size.bit_length() - 1):
        kept = add(kept, swap(kept, bit, size))
    pieces = [kept]
    for bit in (2, 1, 0):
        pieces = pieces + [swap(piece, bit, size) for piece in pieces]
    return pieces


def widen_kernel(bits_ref, *refs):
    for index in range(8):

        @pl.when(pl.program_id(0) == index)
        def _():
            refs[-1][...] = refs[index][...].astype(WIDE)


def widen(bits, pieces, shape, block, place):
    def out_place(r, s):
        q = r ^ (s[0] * 4 + s[1] * 2 + s[2])
        return place(q // 4, (q // 2) % 2, q % 2)

    piece = pieces[0].shape
    return pl.pallas_call(
        widen_kernel,
        grid_spec=pltpu.PrefetchScalarGridSpec(
            num_scalar_prefetch=1,
            grid=(8,),
            in_specs=[pl.BlockSpec(piece, lambda r, s: (0,) * len(piece))] * 8,
            out_specs=pl.BlockSpec(block, out_place),
        ),
        out_shape=jax.ShapeDtypeStruct(shape, WIDE),
        name="widen",
    )(bits, *pieces)


def widen_heads_kernel(bits_ref, *refs):
    for index in range(8):

        @pl.when(pl.program_id(0) == index)
        def _():
            refs[-2][...] = refs[index][:3].astype(WIDE)
            refs[-1][...] = refs[index][3].astype(WIDE)


def widen_heads(bits, pieces, width, local):
    def bits_of(r, s):
        q = r ^ (s[0] * 4 + s[1] * 2 + s[2])
        return q // 4, q % 4

    piece = pieces[0].shape
    return pl.pallas_call(
        widen_heads_kernel,
        grid_spec=pltpu.PrefetchScalarGridSpec(
            num_scalar_prefetch=1,
            grid=(8,),
            in_specs=[pl.BlockSpec(piece, lambda r, s: (0,) * len(piece))] * 8,
            out_specs=[
                pl.BlockSpec((3,) + piece[1:], lambda r, s: (0, bits_of(r, s)[0] * 4 + bits_of(r, s)[1], 0)),
                pl.BlockSpec(piece[1:], lambda r, s: (bits_of(r, s)[1], bits_of(r, s)[0])),
            ],
        ),
        out_shape=[
            jax.ShapeDtypeStruct((3, width, local), WIDE),
            jax.ShapeDtypeStruct((local, width), WIDE),
        ],
        name="widen_heads",
    )(bits, *pieces)


def normalize(values):
    average = jnp.mean(values, axis=-1, keepdims=True)
    centred = values - average
    scale = lax.rsqrt(jnp.mean(centred * centred, axis=-1, keepdims=True) + EPSILON)
    return centred * scale, scale


def normalize_back(grad, normed, scale, gain):
    grad_normed = grad * gain
    first = jnp.mean(grad_normed, axis=-1, keepdims=True)
    second = jnp.mean(grad_normed * normed, axis=-1, keepdims=True)
    return scale * (grad_normed - first - normed * second)


def gelu_pair(values):
    below = 0.5 * lax.erfc(-values * RSQRT2)
    density = RSQRT2PI * jnp.exp(-0.5 * values * values)
    return values * below, below + values * density


def fetch(half, axis, core, size):
    extent = half.shape[axis] // 2
    part = lax.dynamic_slice_in_dim(half, core * extent, extent, axis)
    mine = across(part)
    theirs = swap(mine, 0, size)
    return jnp.where(
        core == 0,
        jnp.concatenate([mine, theirs], axis),
        jnp.concatenate([theirs, mine], axis),
    )


def body(
    tokens,
    lengths,
    w_qkv,
    q_bias,
    v_bias,
    w_out,
    out_bias,
    gain_one,
    shift_one,
    w_in,
    in_bias,
    w_down,
    down_bias,
    gain_two,
    shift_two,
    cotangent,
):
    rows, width = cotangent.shape
    seq_len = tokens.shape[0] // lengths.shape[0]
    sequences = rows // seq_len
    local = w_qkv.shape[2]
    hidden = w_in.shape[1]
    size = lax.axis_size("dp")
    pair = lax.axis_index("tensor")
    dp = lax.axis_index("dp")
    core = dp & 1
    bits = jnp.stack(halves(dp)).astype(jnp.int32)

    x = lax.dynamic_slice_in_dim(tokens, pair * rows, rows, 0)
    own_lengths = lax.dynamic_slice_in_dim(lengths, pair * sequences, sequences, 0)

    qkv_own = jnp.transpose(w_qkv, (1, 0, 2))
    qkv_other = fetch(qkv_own, 1, core, size)
    biases = jnp.concatenate([q_bias, v_bias, in_bias])
    biases_other = across(biases)
    out_other = fetch(w_out, 0, core, size)
    in_other = fetch(w_in, 1, core, size)
    down_other = fetch(w_down, 0, core, size)

    def project(weights, biases):
        q = (jnp.dot(x, weights[0], preferred_element_type=WIDE) + biases[:local]).astype(LOW)
        k = jnp.dot(x, weights[1], preferred_element_type=WIDE).astype(LOW)
        v = (jnp.dot(x, weights[2], preferred_element_type=WIDE) + biases[local : 2 * local]).astype(LOW)
        return q * HEAD_DIM**-0.5, k, v

    q_own, k_own, v_own = project(qkv_own, biases)
    context_own, probs_own = attend(own_lengths, q_own, k_own, v_own)
    q_other, k_other, v_other = project(qkv_other, biases_other)
    context_other, probs_other = attend(own_lengths, q_other, k_other, v_other)

    pre_one = (
        jnp.dot(context_own, w_out, preferred_element_type=WIDE)
        + jnp.dot(context_other, out_other, preferred_element_type=WIDE)
        + out_bias
        + x.astype(WIDE)
    )
    normed_one, scale_one = normalize(pre_one)
    hidden_one = normed_one * gain_one + shift_one
    hidden_low = hidden_one.astype(LOW)

    def expand(weights, bias):
        act, slope = gelu_pair(jnp.dot(hidden_low, weights, preferred_element_type=WIDE) + bias)
        return act.astype(LOW), slope.astype(LOW)

    act_own, slope_own = expand(w_in, in_bias)
    act_other, slope_other = expand(in_other, biases_other[2 * local :])
    pre_two = (
        jnp.dot(act_own, w_down, preferred_element_type=WIDE)
        + jnp.dot(act_other, down_other, preferred_element_type=WIDE)
        + down_bias
        + hidden_one
    )
    normed_two, scale_two = normalize(pre_two)
    output = (normed_two * gain_two + shift_two).astype(LOW)

    cot = cotangent.astype(WIDE)
    grad_gain_two = jnp.sum(cot * normed_two, axis=0)
    grad_shift_two = jnp.sum(cot, axis=0)
    grad_pre_two = normalize_back(cot, normed_two, scale_two, gain_two)
    grad_down_bias = jnp.sum(grad_pre_two, axis=0)
    branch_grad = grad_pre_two.astype(LOW)

    def pieces_of(make, other, own):
        sent = swap(make(bits, 1, *other), 0, size)
        other_sum = make(bits, 0, *other, sent)
        sent = swap(make(bits, 1, *own), 0, size)
        own_sum = make(bits, 0, *own, sent)
        return sum_pieces(own_sum, other_sum, size)

    down_grads = pieces_of(down_pieces, (act_other, branch_grad), (act_own, branch_grad))

    def shrink(weights, slope):
        grad_act = contract(branch_grad, weights, 1, 1)
        grad = (grad_act * slope.astype(WIDE)).astype(LOW)
        return grad, jnp.sum(grad.astype(WIDE), axis=0)

    grad_act_other, in_bias_other = shrink(down_other, slope_other)
    grad_act_own, in_bias_own = shrink(w_down, slope_own)
    in_grads = pieces_of(up_pieces, (hidden_low, grad_act_other), (hidden_low, grad_act_own))

    grad_hidden = (
        contract(grad_act_own, w_in, 1, 1) + contract(grad_act_other, in_other, 1, 1) + grad_pre_two
    )
    grad_gain_one = jnp.sum(grad_hidden * normed_one, axis=0)
    grad_shift_one = jnp.sum(grad_hidden, axis=0)
    grad_pre_one = normalize_back(grad_hidden, normed_one, scale_one, gain_one)
    grad_out_bias = jnp.sum(grad_pre_one, axis=0)
    attended_grad = grad_pre_one.astype(LOW)

    def sum_vectors(shared, own, other):
        count = shared.shape[0]
        arrived = across(jnp.concatenate([shared, other]))
        total = jnp.concatenate([shared, own]) + arrived
        for bit in range(size.bit_length() - 1):
            total = total + swap(total, bit, size)
        return total[:count], total[count:]

    shared, grad_in_bias = sum_vectors(
        jnp.concatenate(
            [grad_out_bias, grad_gain_one, grad_shift_one, grad_down_bias, grad_gain_two, grad_shift_two]
        ),
        in_bias_own,
        in_bias_other,
    )
    shared = shared.reshape(6, width)

    context_grad_other = contract(attended_grad, out_other, 1, 1).astype(LOW)
    project_other = attend_back(
        q_other, k_other, v_other, context_other, context_grad_other, probs_other, sequences
    )
    context_grad_own = contract(attended_grad, w_out, 1, 1).astype(LOW)
    project_own = attend_back(q_own, k_own, v_own, context_own, context_grad_own, probs_own, sequences)

    def outer_pieces(bits, send, grads, context, *received):
        pieces = heads_pieces(bits, send, x, grads, context, attended_grad, *received)
        return pieces

    def heads_make(bits, send, grads, context, *received):
        flat = [r.reshape(4, *r.shape[2:]) for r in received]
        out = outer_pieces(bits, send, grads, context, *flat)
        return out.reshape(2, 2, *out.shape[1:])

    heads_grads = pieces_of(
        heads_make, (project_other, context_other), (project_own, context_own)
    )

    def bias_sums(grads):
        return jnp.concatenate(
            [jnp.sum(grads[0].astype(WIDE), axis=0), jnp.sum(grads[2].astype(WIDE), axis=0)]
        )

    _, head_biases = sum_vectors(
        jnp.zeros((0,), WIDE), bias_sums(project_own), bias_sums(project_other)
    )

    input_grad = grad_pre_one
    for grads, weights in ((project_own, qkv_own), (project_other, qkv_other)):
        for index in range(3):
            input_grad = input_grad + contract(grads[index], weights[index], 1, 1)

    grad_w_down = widen(
        bits, down_grads, (hidden, width), down_grads[0].shape, lambda c, i, z: (c * 4 + i * 2 + z, 0)
    )
    grad_w_in = widen(
        bits, in_grads, (width, hidden), in_grads[0].shape, lambda c, i, z: (z, c * 2 + i)
    )
    grad_qkv, grad_w_out = widen_heads(bits, heads_grads, width, local)

    return (
        output,
        input_grad.astype(LOW),
        jnp.transpose(grad_qkv, (1, 0, 2)),
        head_biases[:local],
        head_biases[local:],
        grad_w_out,
        shared[0],
        shared[1],
        shared[2],
        grad_w_in,
        grad_in_bias,
        grad_w_down,
        shared[3],
        shared[4],
        shared[5],
    )


def solution(mesh):
    placed = (
        P("dp", None),
        P("dp"),
        P(None, None, "tensor"),
        P("tensor"),
        P("tensor"),
        P("tensor", None),
        P(),
        P(),
        P(),
        P(None, "tensor"),
        P("tensor"),
        P("tensor", None),
        P(),
        P(),
        P(),
        P(("dp", "tensor"), None),
    )
    return jax.shard_map(
        body,
        mesh=mesh,
        in_specs=placed,
        out_specs=(
            P(("dp", "tensor"), None),
            P(("dp", "tensor"), None),
            P(None, None, "tensor"),
            P("tensor"),
            P("tensor"),
            P("tensor", None),
            P(),
            P(),
            P(),
            P(None, "tensor"),
            P("tensor"),
            P("tensor", None),
            P(),
            P(),
            P(),
        ),
        check_vma=False,
    )
```

```python
import jax
import jax.numpy as jnp
from jax import lax
from jax.experimental import pallas as pl
from jax.experimental.pallas import tpu as pltpu
from jax.sharding import PartitionSpec as P

HEAD_DIM = 64
EPSILON = 1e-06
MASKED = -1000000000.0
LOW = jnp.bfloat16
WIDE = jnp.float32
RSQRT2PI = 0.3989422804014327


def contract(a, b, dim_a, dim_b):
    return lax.dot_general(
        a, b, (((dim_a,), (dim_b,)), ((), ())), preferred_element_type=WIDE
    )


def halves(d):
    return d & 1, (d >> 1) & 1, (d >> 2) & 1


def swap(array, bit, size):
    return lax.ppermute(array, "dp", [(i, i ^ (1 << bit)) for i in range(size)])


def across(array):
    return lax.ppermute(array, "tensor", [(0, 1), (1, 0)])


def attend_kernel(length_ref, q_ref, k_ref, v_ref, context_ref, probs_ref):
    length = length_ref[pl.program_id(0)]
    rows = q_ref.shape[0]
    lane = lax.broadcasted_iota(jnp.int32, (rows, 128), 1)
    slot = lax.broadcasted_iota(jnp.int32, (rows, 128), 0)
    masked = jnp.where(slot < length, 0.0, MASKED).astype(LOW)
    q, k, v = q_ref[...], k_ref[...], v_ref[...]
    zero, one = jnp.zeros_like(q), jnp.ones_like(q)
    contexts = []
    for head in range(2):
        mine = (lane >= 64) if head else (lane < 64)
        mark = lane == (0 if head else 64)
        k_head = jnp.where(mine, k, jnp.where(mark, masked, zero))
        q_head = jnp.where(mine, q, jnp.where(mark, one, zero))
        scores = contract(k_head, q_head, 1, 1)
        top = jnp.max(scores, axis=0, keepdims=True)
        exponent = jnp.exp(scores - top)
        total = jnp.sum(exponent, axis=0, keepdims=True)
        probs = (exponent * (1.0 / total)).astype(LOW)
        probs_ref[head] = probs
        contexts.append(contract(probs, v, 0, 0))
    context_ref[...] = jnp.where(lane < 64, contexts[0], contexts[1]).astype(LOW)


def attend(lengths, q, k, v):
    rows, width = q.shape
    sequences = lengths.shape[0]
    length, pairs = rows // sequences, width // 128
    block = pl.BlockSpec((length, 128), lambda s, h, *_: (s, h))
    return pl.pallas_call(
        attend_kernel,
        grid_spec=pltpu.PrefetchScalarGridSpec(
            num_scalar_prefetch=1,
            grid=(sequences, pairs),
            in_specs=[block] * 3,
            out_specs=[
                block,
                pl.BlockSpec((2, length, length), lambda s, h, *_: (s * pairs + h, 0, 0)),
            ],
        ),
        out_shape=[
            jax.ShapeDtypeStruct((rows, width), LOW),
            jax.ShapeDtypeStruct((sequences * pairs * 2, length, length), LOW),
        ],
        cost_estimate=small_cost(),
        name="attend",
    )(lengths, q, k, v)


def attend_back_kernel(q_ref, k_ref, v_ref, context_ref, grad_ref, probs_ref, out_ref):
    rows = q_ref.shape[0]
    lane = lax.broadcasted_iota(jnp.int32, (rows, 128), 1)
    q, k, v, grad = q_ref[...], k_ref[...], v_ref[...], grad_ref[...]
    inner = pltpu.roll(grad.astype(WIDE) * context_ref[...].astype(WIDE), 64, 1).astype(LOW)
    zero, minus = jnp.zeros_like(q), -jnp.ones_like(q)
    grad_q = grad_k = grad_v = 0.0
    for head in range(2):
        mine = (lane >= 64) if head else (lane < 64)
        centred = contract(jnp.where(mine, v, minus), jnp.where(mine, grad, inner), 1, 1)
        probs = probs_ref[head]
        grad_scores = (probs.astype(WIDE) * centred).astype(LOW)
        grad_v += contract(probs, jnp.where(mine, grad, zero), 1, 0)
        grad_k += contract(grad_scores, jnp.where(mine, q, zero), 1, 0)
        grad_q += contract(grad_scores, jnp.where(mine, k, zero), 0, 0)
    out_ref[0] = (grad_q * HEAD_DIM**-0.5).astype(LOW)
    out_ref[1] = grad_k.astype(LOW)
    out_ref[2] = grad_v.astype(LOW)


def attend_back(q, k, v, context, grad, probs, sequences):
    rows, width = q.shape
    length, pairs = rows // sequences, width // 128
    block = pl.BlockSpec((length, 128), lambda s, h: (s, h))
    return pl.pallas_call(
        attend_back_kernel,
        grid=(sequences, pairs),
        in_specs=[block] * 5
        + [pl.BlockSpec((2, length, length), lambda s, h: (s * pairs + h, 0, 0))],
        out_specs=pl.BlockSpec((3, length, 128), lambda s, h: (0, s, h)),
        out_shape=jax.ShapeDtypeStruct((3, rows, width), LOW),
        cost_estimate=small_cost(),
        name="attend_back",
    )(q, k, v, context, grad, probs)


def fetch(piece, size):
    here = across(piece)
    pieces = [here, swap(here, 2, size), swap(here, 1, size)]
    pieces.append(swap(pieces[1], 1, size))
    return pieces + [swap(part, 0, size) for part in pieces]


def rank_of(bits_ref):
    return bits_ref[0] * 4 + bits_ref[1] * 2 + bits_ref[2]


class Loads:
    def __init__(self, semaphores):
        self.semaphores, self.count, self.groups = semaphores, 0, []

    def group(self, pairs):
        copies = []
        for source, target in pairs:
            copies.append(pltpu.make_async_copy(source, target, self.semaphores.at[self.count]))
            self.count += 1
        self.groups.append(copies)
        return len(self.groups) - 1

    def start(self):
        @pl.when(pl.program_id(0) == 0)
        def _():
            for copies in self.groups:
                for copy in copies:
                    copy.start()

    def wait(self, group):
        @pl.when(pl.program_id(0) == 0)
        def _():
            for copy in self.groups[group]:
                copy.wait()


def tall(ref, start, extent):
    return ref.at[pl.ds(pl.multiple_of(start, 16), extent)]


def qkv_parts(parts, target, rank):
    extent = target.shape[1] // 8
    return [
        (part.at[:3], target.at[:, pl.ds(pl.multiple_of((r ^ rank) * extent, 16), extent)])
        for r, part in enumerate(parts)
    ]


def out_parts(parts, target, rank):
    extent, width = target.shape[0] // 8, target.shape[1] // 2
    return [
        (
            part.at[3, pl.ds(side * extent, extent)],
            target.at[pl.ds(pl.multiple_of((r ^ rank) * extent, 16), extent), pl.ds(side * width, width)],
        )
        for r, part in enumerate(parts)
        for side in range(2)
    ]


def in_parts(parts, target, rank):
    extent, width = target.shape[0] // 8, target.shape[1] // 2
    return [
        (
            part.at[pl.ds(side * extent, extent)],
            target.at[pl.ds(pl.multiple_of((r ^ rank) * extent, 16), extent), pl.ds(side * width, width)],
        )
        for r, part in enumerate(parts)
        for side in range(2)
    ]


def down_parts(parts, target, rank):
    extent = target.shape[0] // 8
    return [
        (part.at[pl.ds(extent, extent)], target.at[pl.ds(pl.multiple_of((r ^ rank) * extent, 16), extent)])
        for r, part in enumerate(parts)
    ]


ANYWHERE = pl.BlockSpec(memory_space=pl.ANY)


def small_cost(flops=10**6):
    return pl.CostEstimate(flops=flops, bytes_accessed=10**5, transcendentals=0)


def project_kernel(bits_ref, x_ref, q_bias_ref, v_bias_ref, *refs):
    parts, (q_ref, k_ref, v_ref, weights, semaphores) = refs[:-5], refs[-5:]
    loads = Loads(semaphores)
    if len(parts) == 1:
        ready = loads.group([(parts[0], weights)])
    else:
        ready = loads.group(qkv_parts(parts, weights, rank_of(bits_ref)))
    loads.start()
    loads.wait(ready)
    x = x_ref[...]
    queries = (contract(x, weights[0], 1, 0) + q_bias_ref[...]).astype(LOW)
    q_ref[...] = queries * HEAD_DIM**-0.5
    k_ref[...] = contract(x, weights[1], 1, 0).astype(LOW)
    v_ref[...] = (contract(x, weights[2], 1, 0) + v_bias_ref[...]).astype(LOW)


def project(bits, tokens, row_start, rows, local, biases, parts):
    width = tokens.shape[1]
    tile = 256
    return pl.pallas_call(
        project_kernel,
        grid_spec=pltpu.PrefetchScalarGridSpec(
            num_scalar_prefetch=1,
            grid=(rows // tile,),
            in_specs=[
                pl.BlockSpec((tile, width), lambda i, s: (i, 0)),
                pl.BlockSpec((1, local), lambda i, s: (0, 0)),
                pl.BlockSpec((1, local), lambda i, s: (0, 1)),
            ]
            + [ANYWHERE] * len(parts),
            out_specs=[pl.BlockSpec((tile, local), lambda i, s: (i, 0))] * 3,
            scratch_shapes=[pltpu.VMEM((3, width, local), LOW), pltpu.SemaphoreType.DMA((8,))],
        ),
        out_shape=[jax.ShapeDtypeStruct((rows, local), LOW)] * 3,
        cost_estimate=small_cost(),
        name="project",
    )(bits, tokens, biases, biases, *parts)


def project_back_kernel(bits_ref, own_ref, other_ref, grad_ref, weights_ref, *refs):
    parts, (out_ref, own_weights, other_weights, semaphores) = refs[:-4], refs[-4:]
    loads = Loads(semaphores)
    own_ready = loads.group([(weights_ref, own_weights)])
    other_ready = loads.group(qkv_parts(parts, other_weights, rank_of(bits_ref)))
    loads.start()
    loads.wait(own_ready)
    total = grad_ref[...].astype(WIDE)
    for index in range(3):
        total += contract(own_ref[index], own_weights[index], 1, 1)
    loads.wait(other_ready)
    for index in range(3):
        total += contract(other_ref[index], other_weights[index], 1, 1)
    out_ref[...] = total.astype(LOW)


def project_back(bits, own, other, grad, weights, parts):
    rows, width = grad.shape
    local = own.shape[2]
    tile = 256
    block = pl.BlockSpec((3, tile, local), lambda i, s: (0, i, 0))
    row_block = pl.BlockSpec((tile, width), lambda i, s: (i, 0))
    return pl.pallas_call(
        project_back_kernel,
        grid_spec=pltpu.PrefetchScalarGridSpec(
            num_scalar_prefetch=1,
            grid=(rows // tile,),
            in_specs=[block, block, row_block] + [ANYWHERE] * (1 + len(parts)),
            out_specs=row_block,
            scratch_shapes=[pltpu.VMEM((3, width, local), LOW)] * 2 + [pltpu.SemaphoreType.DMA((9,))],
        ),
        out_shape=jax.ShapeDtypeStruct((rows, width), LOW),
        cost_estimate=small_cost(),
        name="project_back",
    )(bits, own, other, grad, weights, *parts)


def normalize(values):
    average = jnp.mean(values, axis=-1, keepdims=True)
    centred = values - average
    scale = lax.rsqrt(jnp.mean(centred * centred, axis=-1, keepdims=True) + EPSILON)
    return centred * scale, scale


def normalize_back(grad, normed, scale, gain):
    grad_normed = grad * gain
    first = jnp.mean(grad_normed, axis=-1, keepdims=True)
    second = jnp.mean(grad_normed * normed, axis=-1, keepdims=True)
    return scale * (grad_normed - first - normed * second)


TAIL = (
    0.0356748104095459,
    -0.15720322728157043,
    0.20635373890399933,
    -0.053683843463659286,
    0.12856172025203705,
    0.09991346299648285,
    0.12075395882129669,
    0.11962930113077164,
)


def gelu_pair(values):
    t = 1.0 / (1.0 + 0.3 * jnp.abs(values))
    bell = jnp.exp(-0.5 * (values * values))
    series = TAIL[0]
    for coefficient in TAIL[1:]:
        series = series * t + coefficient
    tail = bell * (t * series)
    below = jnp.where(values < 0.0, tail, 1.0 - tail)
    return values * below, below + RSQRT2PI * (values * bell)


def first_kernel(
    bits_ref,
    own_context_ref,
    other_context_ref,
    x_ref,
    out_bias_ref,
    gain_ref,
    shift_ref,
    down_bias_ref,
    in_bias_ref,
    w_out_ref,
    w_in_ref,
    w_down_ref,
    *refs,
):
    parts = refs[:8]
    hidden_ref, normed_ref, scale_ref, base_ref, act_ref, slope_ref = refs[8:14]
    own_out, other_out, w_in, w_down, semaphores = refs[14:]
    loads = Loads(semaphores)
    out_ready = loads.group([(w_out_ref, own_out)] + out_parts(parts, other_out, rank_of(bits_ref)))
    in_ready = loads.group([(w_in_ref, w_in)])
    down_ready = loads.group([(w_down_ref, w_down)])
    loads.start()
    loads.wait(out_ready)
    pre_one = contract(own_context_ref[...], own_out[...], 1, 0)
    pre_one += contract(other_context_ref[...], other_out[...], 1, 0)
    pre_one += out_bias_ref[...] + x_ref[...].astype(WIDE)
    normed, scale = normalize(pre_one)
    hidden = normed * gain_ref[...] + shift_ref[...]
    hidden_low = hidden.astype(LOW)
    hidden_ref[...] = hidden_low
    normed_ref[...] = normed.astype(LOW)
    scale_ref[...] = scale
    loads.wait(in_ready)
    act, slope = gelu_pair(contract(hidden_low, w_in[...], 1, 0) + in_bias_ref[...])
    act = act.astype(LOW)
    act_ref[...] = act
    slope_ref[...] = slope.astype(LOW)
    loads.wait(down_ready)
    base_ref[...] = hidden + down_bias_ref[...] + contract(act, w_down[...], 1, 0)


def first_half(bits, own_context, other_context, x, vectors, in_bias, w_out, w_in, w_down, parts):
    rows, width = x.shape
    local, hidden = own_context.shape[1], w_in.shape[1]
    tile = 256

    def row_block(columns):
        return pl.BlockSpec((tile, columns), lambda i, s: (i, 0))

    def whole(columns):
        return pl.BlockSpec((1, columns), lambda i, s: (0, 0))

    return pl.pallas_call(
        first_kernel,
        grid_spec=pltpu.PrefetchScalarGridSpec(
            num_scalar_prefetch=1,
            grid=(rows // tile,),
            in_specs=[row_block(local), row_block(local), row_block(width)]
            + [whole(width)] * 4
            + [whole(hidden)]
            + [ANYWHERE] * (3 + len(parts)),
            out_specs=[
                row_block(width),
                row_block(width),
                row_block(1),
                row_block(width),
                row_block(hidden),
                row_block(hidden),
            ],
            scratch_shapes=[
                pltpu.VMEM((local, width), LOW),
                pltpu.VMEM((local, width), LOW),
                pltpu.VMEM((width, hidden), LOW),
                pltpu.VMEM((hidden, width), LOW),
                pltpu.SemaphoreType.DMA((19,)),
            ],
        ),
        out_shape=[
            jax.ShapeDtypeStruct((rows, width), LOW),
            jax.ShapeDtypeStruct((rows, width), LOW),
            jax.ShapeDtypeStruct((rows, 1), WIDE),
            jax.ShapeDtypeStruct((rows, width), WIDE),
            jax.ShapeDtypeStruct((rows, hidden), LOW),
            jax.ShapeDtypeStruct((rows, hidden), LOW),
        ],
        cost_estimate=small_cost(),
        name="first_half",
    )(bits, own_context, other_context, x, *vectors, in_bias, w_out, w_in, w_down, *parts)


def second_kernel(
    bits_ref,
    hidden_ref,
    base_ref,
    cot_ref,
    slope_ref,
    normed_ref,
    scale_ref,
    gain_one_ref,
    gain_two_ref,
    shift_two_ref,
    in_bias_ref,
    w_out_ref,
    w_in_ref,
    w_down_ref,
    *refs,
):
    out_pieces, pieces = refs[:8], refs[8:16]
    output_ref, branch_ref, act_ref, own_grad_ref, other_grad_ref, attended_ref = refs[16:22]
    own_context_ref, other_context_ref, sums_ref, bias_sums_ref = refs[22:26]
    own_out, other_out, own_in, other_in, own_down, other_down, semaphores = refs[26:]
    rank = rank_of(bits_ref)
    loads = Loads(semaphores)
    other_in_ready = loads.group(in_parts(pieces, other_in, rank))
    other_down_ready = loads.group(down_parts(pieces, other_down, rank))
    own_down_ready = loads.group([(w_down_ref, own_down)])
    own_in_ready = loads.group([(w_in_ref, own_in)])
    out_ready = loads.group([(w_out_ref, own_out)] + out_parts(out_pieces, other_out, rank))
    loads.start()

    @pl.when(pl.program_id(0) == 0)
    def _():
        sums_ref[...] = jnp.zeros_like(sums_ref)
        bias_sums_ref[...] = jnp.zeros_like(bias_sums_ref)

    def count(ref, row, values):
        ref[row : row + 1] += jnp.sum(values, axis=0, keepdims=True)

    loads.wait(other_in_ready)
    act, slope = gelu_pair(contract(hidden_ref[...], other_in[...], 1, 0) + in_bias_ref[...])
    act = act.astype(LOW)
    act_ref[...] = act
    loads.wait(other_down_ready)
    pre_two = base_ref[...] + contract(act, other_down[...], 1, 0)
    normed, scale = normalize(pre_two)
    output_ref[...] = (normed * gain_two_ref[...] + shift_two_ref[...]).astype(LOW)
    cot = cot_ref[...].astype(WIDE)
    grad_pre_two = normalize_back(cot, normed, scale, gain_two_ref[...])
    count(sums_ref, 4, cot * normed)
    count(sums_ref, 5, cot)
    count(sums_ref, 3, grad_pre_two)
    branch_grad = grad_pre_two.astype(LOW)
    branch_ref[...] = branch_grad
    grad = contract(branch_grad, other_down[...], 1, 1) * slope
    count(bias_sums_ref, 1, grad)
    grad = grad.astype(LOW)
    other_grad_ref[...] = grad
    grad_hidden = grad_pre_two + contract(grad, other_in[...], 1, 1)
    loads.wait(own_down_ready)
    grad = contract(branch_grad, own_down[...], 1, 1) * slope_ref[...].astype(WIDE)
    count(bias_sums_ref, 0, grad)
    grad = grad.astype(LOW)
    own_grad_ref[...] = grad
    loads.wait(own_in_ready)
    grad_hidden += contract(grad, own_in[...], 1, 1)
    normed = normed_ref[...].astype(WIDE)
    grad_pre_one = normalize_back(grad_hidden, normed, scale_ref[...], gain_one_ref[...])
    count(sums_ref, 1, grad_hidden * normed)
    count(sums_ref, 2, grad_hidden)
    count(sums_ref, 0, grad_pre_one)
    attended = grad_pre_one.astype(LOW)
    attended_ref[...] = attended
    loads.wait(out_ready)
    own_context_ref[...] = contract(attended, own_out[...], 1, 1).astype(LOW)
    other_context_ref[...] = contract(attended, other_out[...], 1, 1).astype(LOW)


def second_half(bits, hidden_low, base, cot, slope, normed, scale, vectors, in_bias, w_out, w_in, w_down, out_pieces, pieces):
    rows, width = hidden_low.shape
    local, hidden = w_out.shape[0], w_in.shape[1]
    tile = 256

    def row_block(columns):
        return pl.BlockSpec((tile, columns), lambda i, s: (i, 0))

    def whole(columns, count=1):
        return pl.BlockSpec((count, columns), lambda i, s: (0, 0))

    def low(columns):
        return jax.ShapeDtypeStruct((rows, columns), LOW)

    return pl.pallas_call(
        second_kernel,
        grid_spec=pltpu.PrefetchScalarGridSpec(
            num_scalar_prefetch=1,
            grid=(rows // tile,),
            in_specs=[
                row_block(width),
                row_block(width),
                row_block(width),
                row_block(hidden),
                row_block(width),
                row_block(1),
            ]
            + [whole(width)] * 3
            + [whole(hidden)]
            + [ANYWHERE] * 19,
            out_specs=[
                row_block(width),
                row_block(width),
                row_block(hidden),
                row_block(hidden),
                row_block(hidden),
                row_block(width),
                row_block(local),
                row_block(local),
                whole(width, 8),
                whole(hidden, 8),
            ],
            scratch_shapes=[
                pltpu.VMEM((local, width), LOW),
                pltpu.VMEM((local, width), LOW),
                pltpu.VMEM((width, hidden), LOW),
                pltpu.VMEM((width, hidden), LOW),
                pltpu.VMEM((hidden, width), LOW),
                pltpu.VMEM((hidden, width), LOW),
                pltpu.SemaphoreType.DMA((43,)),
            ],
        ),
        out_shape=[
            low(width),
            low(width),
            low(hidden),
            low(hidden),
            low(hidden),
            low(width),
            low(local),
            low(local),
            jax.ShapeDtypeStruct((8, width), WIDE),
            jax.ShapeDtypeStruct((8, hidden), WIDE),
        ],
        cost_estimate=small_cost(),
        name="second_half",
    )(bits, hidden_low, base, cot, slope, normed, scale, *vectors, in_bias, w_out, w_in, w_down, *out_pieces, *pieces)


def down_kernel(bits_ref, act_ref, grad_ref, sent_ref, kept_ref):
    z = bits_ref[2]
    result = contract(act_ref[...], grad_ref[...], 0, 0)
    rows = result.shape[0] // 2

    def put(out_ref):
        for part in range(2):
            out_ref[0, part ^ z] = result[part * rows : (part + 1) * rows].astype(LOW)

    @pl.when(pl.program_id(0) < 2)
    def _():
        put(sent_ref)

    @pl.when(pl.program_id(0) >= 2)
    def _():
        put(kept_ref)


def down_pieces(bits, activated, grad):
    rows, hidden = activated.shape
    width = grad.shape[1]
    piece = (1, 2, hidden // 8, width)
    return pl.pallas_call(
        down_kernel,
        grid_spec=pltpu.PrefetchScalarGridSpec(
            num_scalar_prefetch=1,
            grid=(4,),
            in_specs=[
                pl.BlockSpec(
                    (rows, hidden // 4), lambda i, s: (0, (s[0] ^ (1 - i // 2)) * 2 + ((i % 2) ^ s[1]))
                ),
                pl.BlockSpec((rows, width), lambda i, s: (0, 0)),
            ],
            out_specs=[
                pl.BlockSpec(piece, lambda i, s: (jnp.minimum(i, 1), 0, 0, 0)),
                pl.BlockSpec(piece, lambda i, s: (jnp.maximum(i - 2, 0), 0, 0, 0)),
            ],
        ),
        out_shape=[jax.ShapeDtypeStruct((2,) + piece[1:], LOW)] * 2,
        cost_estimate=small_cost(),
        name="down_pieces",
    )(bits, activated, grad)


def in_kernel(bits_ref, hidden_ref, grad_ref, sent_ref, kept_ref):
    x, z = bits_ref[1], bits_ref[2]
    result = contract(hidden_ref[...], grad_ref[...], 0, 0)
    rows, columns = result.shape[0] // 2, result.shape[1] // 2

    def put(out_ref):
        for side in range(2):
            for part in range(2):
                out_ref[side ^ x, part ^ z] = result[
                    part * rows : (part + 1) * rows, side * columns : (side + 1) * columns
                ].astype(LOW)

    @pl.when(pl.program_id(0) == 0)
    def _():
        put(sent_ref)

    @pl.when(pl.program_id(0) == 1)
    def _():
        put(kept_ref)


def in_pieces(bits, hidden_low, grad):
    rows, width = hidden_low.shape
    hidden = grad.shape[1]
    piece = (2, 2, width // 2, hidden // 4)
    return pl.pallas_call(
        in_kernel,
        grid_spec=pltpu.PrefetchScalarGridSpec(
            num_scalar_prefetch=1,
            grid=(2,),
            in_specs=[
                pl.BlockSpec((rows, width), lambda i, s: (0, 0)),
                pl.BlockSpec((rows, hidden // 2), lambda i, s: (0, s[0] ^ (1 - i))),
            ],
            out_specs=[pl.BlockSpec(piece, lambda i, s: (0, 0, 0, 0))] * 2,
        ),
        out_shape=[jax.ShapeDtypeStruct(piece, LOW)] * 2,
        cost_estimate=small_cost(),
        name="in_pieces",
    )(bits, hidden_low, grad)


def heads_kernel(bits_ref, x_ref, grads_ref, context_ref, attended_ref, sent_ref, kept_ref, scratch):
    core = bits_ref[0]
    mine = bits_ref[1] * 2 + bits_ref[2]
    extent, local = scratch.shape[1:]

    @pl.when(pl.program_id(0) < 3)
    def _():
        result = contract(x_ref[...], grads_ref[0], 0, 0)
        for part in range(8):
            scratch[part] = result[part * extent : (part + 1) * extent]

    @pl.when(pl.program_id(0) == 3)
    def _():
        result = contract(context_ref[...], attended_ref[...], 0, 0)
        for part in range(8):
            rows, side = part % 4, part // 4
            scratch[part] = result[rows * extent : (rows + 1) * extent, side * local : (side + 1) * local]

    for part in range(4):
        sent_ref[part ^ mine, 0] = scratch[(1 - core) * 4 + part].astype(LOW)
        kept_ref[part ^ mine, 0] = scratch[core * 4 + part].astype(LOW)


def heads_pieces(bits, tokens, grads, context, attended):
    rows, width = tokens.shape
    local = context.shape[1]
    return pl.pallas_call(
        heads_kernel,
        grid_spec=pltpu.PrefetchScalarGridSpec(
            num_scalar_prefetch=1,
            grid=(4,),
            in_specs=[
                pl.BlockSpec((rows, width), lambda j, s: (0, 0)),
                pl.BlockSpec((1, rows, local), lambda j, s: (jnp.minimum(j, 2), 0, 0)),
                pl.BlockSpec((rows, local), lambda j, s: (0, 0)),
                pl.BlockSpec((rows, width), lambda j, s: (0, 0)),
            ],
            out_specs=[pl.BlockSpec((4, 1, width // 8, local), lambda j, s: (0, j, 0, 0))] * 2,
            scratch_shapes=[pltpu.VMEM((8, width // 8, local), WIDE)],
        ),
        out_shape=[jax.ShapeDtypeStruct((4, 4, width // 8, local), LOW)] * 2,
        cost_estimate=small_cost(),
        name="heads_pieces",
    )(bits, tokens, grads, context, attended)


def add(*arrays):
    total = arrays[0].astype(WIDE)
    for array in arrays[1:]:
        total = total + array.astype(WIDE)
    return total.astype(LOW)


def sum_pieces(own, other, size):
    arrived = across(add(other[1], swap(other[0], 0, size)))
    chip = swap(own[0], 0, size)
    there = swap(add(own[1][1], chip[1], arrived[1]), 1, size)
    next_there = swap(add(own[1][0, 1], chip[0, 1], arrived[0, 1], there[1]), 2, size)
    kept = add(own[1][0, 0], chip[0, 0], arrived[0, 0], there[0], next_there)
    for bit in range(3, size.bit_length() - 1):
        kept = add(kept, swap(kept, bit, size))
    pieces = [kept]
    for bit in (2, 1, 0):
        pieces = pieces + [swap(piece, bit, size) for piece in pieces]
    return pieces


def widen_kernel(bits_ref, *refs):
    for index in range(8):

        @pl.when(pl.program_id(0) == index)
        def _():
            refs[-1][...] = refs[index][...].astype(WIDE)


def widen(bits, pieces, shape, block, place):
    def out_place(r, s):
        q = r ^ (s[0] * 4 + s[1] * 2 + s[2])
        return place(q // 4, (q // 2) % 2, q % 2)

    piece = pieces[0].shape
    return pl.pallas_call(
        widen_kernel,
        grid_spec=pltpu.PrefetchScalarGridSpec(
            num_scalar_prefetch=1,
            grid=(8,),
            in_specs=[pl.BlockSpec(piece, lambda r, s: (0,) * len(piece))] * 8,
            out_specs=pl.BlockSpec(block, out_place),
        ),
        out_shape=jax.ShapeDtypeStruct(shape, WIDE),
        name="widen",
    )(bits, *pieces)


def widen_heads_kernel(bits_ref, *refs):
    for index in range(8):

        @pl.when(pl.program_id(0) == index)
        def _():
            refs[-2][...] = refs[index][:3].astype(WIDE)
            refs[-1][...] = refs[index][3].astype(WIDE)


def widen_heads(bits, pieces, width, local):
    def bits_of(r, s):
        q = r ^ (s[0] * 4 + s[1] * 2 + s[2])
        return q // 4, q % 4

    piece = pieces[0].shape
    return pl.pallas_call(
        widen_heads_kernel,
        grid_spec=pltpu.PrefetchScalarGridSpec(
            num_scalar_prefetch=1,
            grid=(8,),
            in_specs=[pl.BlockSpec(piece, lambda r, s: (0,) * len(piece))] * 8,
            out_specs=[
                pl.BlockSpec((3,) + piece[1:], lambda r, s: (0, bits_of(r, s)[0] * 4 + bits_of(r, s)[1], 0)),
                pl.BlockSpec(piece[1:], lambda r, s: (bits_of(r, s)[1], bits_of(r, s)[0])),
            ],
        ),
        out_shape=[
            jax.ShapeDtypeStruct((3, width, local), WIDE),
            jax.ShapeDtypeStruct((local, width), WIDE),
        ],
        name="widen_heads",
    )(bits, *pieces)


def body(
    tokens,
    lengths,
    w_qkv,
    q_bias,
    v_bias,
    w_out,
    out_bias,
    gain_one,
    shift_one,
    w_in,
    in_bias,
    w_down,
    down_bias,
    gain_two,
    shift_two,
    cotangent,
):
    rows, width = cotangent.shape
    seq_len = tokens.shape[0] // lengths.shape[0]
    sequences = rows // seq_len
    local = w_qkv.shape[2]
    hidden = w_in.shape[1]
    size = lax.axis_size("dp")
    pair = lax.axis_index("tensor")
    dp = lax.axis_index("dp")
    bits = jnp.stack(halves(dp)).astype(jnp.int32)
    rank = (dp & 1) * 4 + ((dp >> 1) & 1) * 2 + ((dp >> 2) & 1)

    def row(vector):
        return vector.reshape(1, -1)

    def eighth(array, axis):
        extent = array.shape[axis] // 8
        return lax.dynamic_slice_in_dim(array, rank * extent, extent, axis)

    def stacked(array):
        columns = array.shape[1] // 2
        return jnp.concatenate([array[:, :columns], array[:, columns:]], axis=0)

    qkv_own = jnp.transpose(w_qkv, (1, 0, 2))
    attention_pieces = fetch(
        jnp.concatenate([eighth(qkv_own, 1), stacked(eighth(w_out, 0))[None]], axis=0), size
    )
    biases = jnp.concatenate([q_bias, v_bias, in_bias])
    biases_other = across(biases)
    forward_pieces = fetch(
        jnp.concatenate([stacked(eighth(w_in, 0)), eighth(w_down, 0)], axis=0), size
    )

    x = lax.dynamic_slice_in_dim(tokens, pair * rows, rows, 0)
    own_lengths = lax.dynamic_slice_in_dim(lengths, pair * sequences, sequences, 0)

    q_own, k_own, v_own = project(bits, x, 0, rows, local, row(biases[: 2 * local]), [qkv_own])
    context_own, probs_own = attend(own_lengths, q_own, k_own, v_own)
    q_other, k_other, v_other = project(
        bits, x, 0, rows, local, row(biases_other[: 2 * local]), attention_pieces
    )
    context_other, probs_other = attend(own_lengths, q_other, k_other, v_other)

    hidden_low, normed_one, scale_one, base, act_own, slope_own = first_half(
        bits,
        context_own,
        context_other,
        x,
        [row(out_bias), row(gain_one), row(shift_one), row(down_bias)],
        row(in_bias),
        w_out,
        w_in,
        w_down,
        attention_pieces,
    )
    (
        output,
        branch_grad,
        act_other,
        grad_own,
        grad_other,
        attended_grad,
        context_grad_own,
        context_grad_other,
        sums,
        bias_sums,
    ) = second_half(
        bits,
        hidden_low,
        base,
        cotangent,
        slope_own,
        normed_one,
        scale_one,
        [row(gain_one), row(gain_two), row(shift_two)],
        row(biases_other[2 * local :]),
        w_out,
        w_in,
        w_down,
        attention_pieces,
        forward_pieces,
    )

    down_grads = sum_pieces(
        down_pieces(bits, act_own, branch_grad), down_pieces(bits, act_other, branch_grad), size
    )
    in_grads = sum_pieces(
        in_pieces(bits, hidden_low, grad_own), in_pieces(bits, hidden_low, grad_other), size
    )

    def sum_vectors(shared, own, other):
        count = shared.shape[0]
        arrived = across(jnp.concatenate([shared, other]))
        total = jnp.concatenate([shared, own]) + arrived
        for bit in range(size.bit_length() - 1):
            total = total + swap(total, bit, size)
        return total[:count], total[count:]

    shared, grad_in_bias = sum_vectors(sums[:6].reshape(-1), bias_sums[0], bias_sums[1])
    shared = shared.reshape(6, width)

    def heads_back(q, k, v, context, context_grad, probs):
        grads = attend_back(q, k, v, context, context_grad, probs, sequences)
        pieces = heads_pieces(bits, x, grads, context, attended_grad)
        return grads, [piece.reshape(2, 2, *piece.shape[1:]) for piece in pieces]

    project_other, heads_other = heads_back(
        q_other, k_other, v_other, context_other, context_grad_other, probs_other
    )
    project_own, heads_own = heads_back(q_own, k_own, v_own, context_own, context_grad_own, probs_own)
    heads_grads = sum_pieces(heads_own, heads_other, size)

    def head_sums(grads):
        return jnp.concatenate(
            [jnp.sum(grads[0].astype(WIDE), axis=0), jnp.sum(grads[2].astype(WIDE), axis=0)]
        )

    _, head_biases = sum_vectors(
        jnp.zeros((0,), WIDE), head_sums(project_own), head_sums(project_other)
    )

    input_grad = project_back(bits, project_own, project_other, attended_grad, qkv_own, attention_pieces)

    grad_w_down = widen(
        bits, down_grads, (hidden, width), down_grads[0].shape, lambda c, i, z: (c * 4 + i * 2 + z, 0)
    )
    grad_w_in = widen(
        bits, in_grads, (width, hidden), in_grads[0].shape, lambda c, i, z: (z, c * 2 + i)
    )
    grad_qkv, grad_w_out = widen_heads(bits, heads_grads, width, local)

    return (
        output,
        input_grad,
        jnp.transpose(grad_qkv, (1, 0, 2)),
        head_biases[:local],
        head_biases[local:],
        grad_w_out,
        shared[0],
        shared[1],
        shared[2],
        grad_w_in,
        grad_in_bias,
        grad_w_down,
        shared[3],
        shared[4],
        shared[5],
    )


def solution(mesh):
    placed = (
        P("dp", None),
        P("dp"),
        P(None, None, "tensor"),
        P("tensor"),
        P("tensor"),
        P("tensor", None),
        P(),
        P(),
        P(),
        P(None, "tensor"),
        P("tensor"),
        P("tensor", None),
        P(),
        P(),
        P(),
        P(("dp", "tensor"), None),
    )
    return jax.shard_map(
        body,
        mesh=mesh,
        in_specs=placed,
        out_specs=(
            P(("dp", "tensor"), None),
            P(("dp", "tensor"), None),
            P(None, None, "tensor"),
            P("tensor"),
            P("tensor"),
            P("tensor", None),
            P(),
            P(),
            P(),
            P(None, "tensor"),
            P("tensor"),
            P("tensor", None),
            P(),
            P(),
            P(),
        ),
        check_vma=False,
    )
```

```python
import jax
import jax.numpy as jnp
from jax import lax
from jax.experimental import pallas as pl
from jax.experimental.pallas import tpu as pltpu
from jax.sharding import PartitionSpec as P

HEAD_DIM = 64
EPSILON = 1e-06
MASKED = -1000000000.0
LOW = jnp.bfloat16
WIDE = jnp.float32
RSQRT2PI = 0.3989422804014327


def contract(a, b, dim_a, dim_b):
    return lax.dot_general(
        a, b, (((dim_a,), (dim_b,)), ((), ())), preferred_element_type=WIDE
    )


def halves(d):
    return d & 1, (d >> 1) & 1, (d >> 2) & 1


def swap(array, bit, size):
    return lax.ppermute(array, "dp", [(i, i ^ (1 << bit)) for i in range(size)])


def across(array):
    return lax.ppermute(array, "tensor", [(0, 1), (1, 0)])


ANYWHERE = pl.BlockSpec(memory_space=pl.ANY)


def small_cost(flops=10**6):
    return pl.CostEstimate(flops=flops, bytes_accessed=10**5, transcendentals=0)


def attend_kernel(length_ref, sequence, q_ref, k_ref, v_ref, context_ref, probs_ref):
    length = length_ref[sequence]
    rows = q_ref.shape[0]
    lane = lax.broadcasted_iota(jnp.int32, (rows, 128), 1)
    slot = lax.broadcasted_iota(jnp.int32, (rows, 128), 0)
    masked = jnp.where(slot < length, 0.0, MASKED).astype(LOW)
    q, k, v = q_ref[...], k_ref[...], v_ref[...]
    zero, one = jnp.zeros_like(q), jnp.ones_like(q)
    contexts = []
    for head in range(2):
        mine = (lane >= 64) if head else (lane < 64)
        mark = lane == (0 if head else 64)
        k_head = jnp.where(mine, k, jnp.where(mark, masked, zero))
        q_head = jnp.where(mine, q, jnp.where(mark, one, zero))
        scores = contract(k_head, q_head, 1, 1)
        top = jnp.max(scores, axis=0, keepdims=True)
        exponent = jnp.exp(scores - top)
        total = jnp.sum(exponent, axis=0, keepdims=True)
        probs = (exponent * (1.0 / total)).astype(LOW)
        probs_ref[head] = probs
        contexts.append(contract(probs, v, 0, 0))
    context_ref[...] = jnp.where(lane < 64, contexts[0], contexts[1]).astype(LOW)


def attend(lengths, q, k, v, sequence, *begun):
    rows, width = q.shape
    sequences = lengths.shape[0]
    length, pairs = rows // sequences, width // 128
    block = pl.BlockSpec((length, 128), lambda s, h, *_: (sequence, h))

    def kernel(length_ref, *refs):
        attend_kernel(length_ref, sequence, *refs[:3], *refs[-2:])

    return pl.pallas_call(
        kernel,
        grid_spec=pltpu.PrefetchScalarGridSpec(
            num_scalar_prefetch=1,
            grid=(1, pairs),
            in_specs=[block] * 3 + [ANYWHERE] * len(begun),
            out_specs=[
                block,
                pl.BlockSpec((2, length, length), lambda s, h, *_: (sequence * pairs + h, 0, 0)),
            ],
        ),
        out_shape=[
            jax.ShapeDtypeStruct((rows, width), LOW),
            jax.ShapeDtypeStruct((sequences * pairs * 2, length, length), LOW),
        ],
        input_output_aliases={4 + i: i for i in range(len(begun))},
        cost_estimate=small_cost(),
        name="attend",
    )(lengths, q, k, v, *begun)


def attend_back_kernel(q_ref, k_ref, v_ref, context_ref, grad_ref, probs_ref, out_ref):
    rows = q_ref.shape[0]
    lane = lax.broadcasted_iota(jnp.int32, (rows, 128), 1)
    q, k, v, grad = q_ref[...], k_ref[...], v_ref[...], grad_ref[...]
    inner = pltpu.roll(grad.astype(WIDE) * context_ref[...].astype(WIDE), 64, 1).astype(LOW)
    zero, minus = jnp.zeros_like(q), -jnp.ones_like(q)
    grad_q = grad_k = grad_v = 0.0
    for head in range(2):
        mine = (lane >= 64) if head else (lane < 64)
        centred = contract(jnp.where(mine, v, minus), jnp.where(mine, grad, inner), 1, 1)
        probs = probs_ref[head]
        grad_scores = (probs.astype(WIDE) * centred).astype(LOW)
        grad_v += contract(probs, jnp.where(mine, grad, zero), 1, 0)
        grad_k += contract(grad_scores, jnp.where(mine, q, zero), 1, 0)
        grad_q += contract(grad_scores, jnp.where(mine, k, zero), 0, 0)
    out_ref[0] = (grad_q * HEAD_DIM**-0.5).astype(LOW)
    out_ref[1] = grad_k.astype(LOW)
    out_ref[2] = grad_v.astype(LOW)


def attend_back(q, k, v, context, grad, probs, sequences):
    rows, width = q.shape
    length, pairs = rows // sequences, width // 128
    block = pl.BlockSpec((length, 128), lambda s, h: (s, h))
    return pl.pallas_call(
        attend_back_kernel,
        grid=(sequences, pairs),
        in_specs=[block] * 5
        + [pl.BlockSpec((2, length, length), lambda s, h: (s * pairs + h, 0, 0))],
        out_specs=pl.BlockSpec((3, length, 128), lambda s, h: (0, s, h)),
        out_shape=jax.ShapeDtypeStruct((3, rows, width), LOW),
        cost_estimate=small_cost(),
        name="attend_back",
    )(q, k, v, context, grad, probs)


class Order:
    def __init__(self, first):
        self.last = first

    def sync(self, *arrays):
        arrays, self.last = lax.optimization_barrier((arrays, self.last))
        return arrays

    def run(self, step, *arrays):
        arrays = self.sync(*arrays)
        result = step(*arrays)
        self.last = result[0] if isinstance(result, (list, tuple)) else result
        return result


class Fetch:
    def __init__(self, order, piece, size):
        self.order, self.size = order, size
        self.here = across(piece)

    def pass_on(self):
        (self.here,) = self.order.sync(self.here)
        self.z, self.x = swap(self.here, 2, self.size), swap(self.here, 1, self.size)
        self.partner = [swap(self.here, 0, self.size)]

    def finish(self):
        self.z, self.x = self.order.sync(self.z, self.x)
        last = swap(self.z, 1, self.size)
        self.partner += [swap(self.z, 0, self.size), swap(self.x, 0, self.size), swap(last, 0, self.size)]
        return [self.here, self.z, self.x, last] + self.partner


def rank_of(bits_ref):
    return bits_ref[0] * 4 + bits_ref[1] * 2 + bits_ref[2]


class Loads:
    def __init__(self, semaphores):
        self.semaphores, self.count, self.groups = semaphores, 0, []

    def group(self, pairs):
        copies = []
        for source, target in pairs:
            copies.append(pltpu.make_async_copy(source, target, self.semaphores.at[self.count]))
            self.count += 1
        self.groups.append(copies)
        return len(self.groups) - 1

    def start(self):
        @pl.when(pl.program_id(0) == 0)
        def _():
            for copies in self.groups:
                for copy in copies:
                    copy.start()

    def wait(self, group):
        @pl.when(pl.program_id(0) == 0)
        def _():
            for copy in self.groups[group]:
                copy.wait()


def tall(ref, start, extent):
    return ref.at[pl.ds(pl.multiple_of(start, 16), extent)]


def qkv_parts(parts, target, rank):
    extent = target.shape[1] // 8
    return [
        (part.at[:3], target.at[:, pl.ds(pl.multiple_of((r ^ rank) * extent, 16), extent)])
        for r, part in enumerate(parts)
    ]


def out_parts(parts, target, rank):
    extent, width = target.shape[0] // 8, target.shape[1] // 2
    return [
        (
            part.at[3, pl.ds(side * extent, extent)],
            target.at[pl.ds(pl.multiple_of((r ^ rank) * extent, 16), extent), pl.ds(side * width, width)],
        )
        for r, part in enumerate(parts)
        for side in range(2)
    ]


def in_parts(parts, target, rank):
    extent, width = target.shape[0] // 8, target.shape[1] // 2
    return [
        (
            part.at[pl.ds(side * extent, extent)],
            target.at[pl.ds(pl.multiple_of((r ^ rank) * extent, 16), extent), pl.ds(side * width, width)],
        )
        for r, part in enumerate(parts)
        for side in range(2)
    ]


def down_parts(parts, target, rank):
    extent = target.shape[0] // 8
    return [
        (part.at[pl.ds(extent, extent)], target.at[pl.ds(pl.multiple_of((r ^ rank) * extent, 16), extent)])
        for r, part in enumerate(parts)
    ]


def project_kernel(bits_ref, x_ref, q_bias_ref, v_bias_ref, *refs):
    parts, (q_ref, k_ref, v_ref, weights, semaphores) = refs[:-5], refs[-5:]
    loads = Loads(semaphores)
    if len(parts) == 1:
        ready = loads.group([(parts[0], weights)])
    else:
        ready = loads.group(qkv_parts(parts, weights, rank_of(bits_ref)))
    loads.start()
    loads.wait(ready)
    x = x_ref[...]
    queries = (contract(x, weights[0], 1, 0) + q_bias_ref[...]).astype(LOW)
    q_ref[...] = queries * HEAD_DIM**-0.5
    k_ref[...] = contract(x, weights[1], 1, 0).astype(LOW)
    v_ref[...] = (contract(x, weights[2], 1, 0) + v_bias_ref[...]).astype(LOW)


def project(bits, tokens, row_start, rows, local, biases, parts):
    width = tokens.shape[1]
    tile = 256
    return pl.pallas_call(
        project_kernel,
        grid_spec=pltpu.PrefetchScalarGridSpec(
            num_scalar_prefetch=1,
            grid=(rows // tile,),
            in_specs=[
                pl.BlockSpec((tile, width), lambda i, s: (i, 0)),
                pl.BlockSpec((1, local), lambda i, s: (0, 0)),
                pl.BlockSpec((1, local), lambda i, s: (0, 1)),
            ]
            + [ANYWHERE] * len(parts),
            out_specs=[pl.BlockSpec((tile, local), lambda i, s: (i, 0))] * 3,
            scratch_shapes=[pltpu.VMEM((3, width, local), LOW), pltpu.SemaphoreType.DMA((8,))],
        ),
        out_shape=[jax.ShapeDtypeStruct((rows, local), LOW)] * 3,
        cost_estimate=small_cost(),
        name="project",
    )(bits, tokens, biases, biases, *parts)


def project_back_kernel(bits_ref, own_ref, other_ref, grad_ref, weights_ref, *refs):
    parts, (out_ref, own_weights, other_weights, semaphores) = refs[:-4], refs[-4:]
    loads = Loads(semaphores)
    own_ready = loads.group([(weights_ref, own_weights)])
    other_ready = loads.group(qkv_parts(parts, other_weights, rank_of(bits_ref)))
    loads.start()
    loads.wait(own_ready)
    total = grad_ref[...].astype(WIDE)
    for index in range(3):
        total += contract(own_ref[index], own_weights[index], 1, 1)
    loads.wait(other_ready)
    for index in range(3):
        total += contract(other_ref[index], other_weights[index], 1, 1)
    out_ref[...] = total.astype(LOW)


def project_back(bits, own, other, grad, weights, parts):
    rows, width = grad.shape
    local = own.shape[2]
    tile = 256
    block = pl.BlockSpec((3, tile, local), lambda i, s: (0, i, 0))
    row_block = pl.BlockSpec((tile, width), lambda i, s: (i, 0))
    return pl.pallas_call(
        project_back_kernel,
        grid_spec=pltpu.PrefetchScalarGridSpec(
            num_scalar_prefetch=1,
            grid=(rows // tile,),
            in_specs=[block, block, row_block] + [ANYWHERE] * (1 + len(parts)),
            out_specs=row_block,
            scratch_shapes=[pltpu.VMEM((3, width, local), LOW)] * 2 + [pltpu.SemaphoreType.DMA((9,))],
        ),
        out_shape=jax.ShapeDtypeStruct((rows, width), LOW),
        cost_estimate=small_cost(),
        name="project_back",
    )(bits, own, other, grad, weights, *parts)


def normalize(values):
    average = jnp.mean(values, axis=-1, keepdims=True)
    centred = values - average
    scale = lax.rsqrt(jnp.mean(centred * centred, axis=-1, keepdims=True) + EPSILON)
    return centred * scale, scale


def normalize_back(grad, normed, scale, gain):
    grad_normed = grad * gain
    first = jnp.mean(grad_normed, axis=-1, keepdims=True)
    second = jnp.mean(grad_normed * normed, axis=-1, keepdims=True)
    return scale * (grad_normed - first - normed * second)


TAIL = (
    0.0356748104095459,
    -0.15720322728157043,
    0.20635373890399933,
    -0.053683843463659286,
    0.12856172025203705,
    0.09991346299648285,
    0.12075395882129669,
    0.11962930113077164,
)


def gelu_pair(values):
    t = 1.0 / (1.0 + 0.3 * jnp.abs(values))
    bell = jnp.exp(-0.5 * (values * values))
    series = TAIL[0]
    for coefficient in TAIL[1:]:
        series = series * t + coefficient
    tail = bell * (t * series)
    below = jnp.where(values < 0.0, tail, 1.0 - tail)
    return values * below, below + RSQRT2PI * (values * bell)


def first_kernel(
    bits_ref,
    own_context_ref,
    other_context_ref,
    x_ref,
    out_bias_ref,
    gain_ref,
    shift_ref,
    down_bias_ref,
    in_bias_ref,
    w_out_ref,
    w_in_ref,
    w_down_ref,
    *refs,
):
    parts = refs[:8]
    hidden_ref, normed_ref, scale_ref, base_ref, act_ref, slope_ref = refs[8:14]
    own_out, other_out, w_in, w_down, semaphores = refs[14:]
    loads = Loads(semaphores)
    out_ready = loads.group([(w_out_ref, own_out)] + out_parts(parts, other_out, rank_of(bits_ref)))
    in_ready = loads.group([(w_in_ref, w_in)])
    down_ready = loads.group([(w_down_ref, w_down)])
    loads.start()
    loads.wait(out_ready)
    pre_one = contract(own_context_ref[...], own_out[...], 1, 0)
    pre_one += contract(other_context_ref[...], other_out[...], 1, 0)
    pre_one += out_bias_ref[...] + x_ref[...].astype(WIDE)
    normed, scale = normalize(pre_one)
    hidden = normed * gain_ref[...] + shift_ref[...]
    hidden_low = hidden.astype(LOW)
    hidden_ref[...] = hidden_low
    normed_ref[...] = normed.astype(LOW)
    scale_ref[...] = scale
    loads.wait(in_ready)
    act, slope = gelu_pair(contract(hidden_low, w_in[...], 1, 0) + in_bias_ref[...])
    act = act.astype(LOW)
    act_ref[...] = act
    slope_ref[...] = slope.astype(LOW)
    loads.wait(down_ready)
    base_ref[...] = hidden + down_bias_ref[...] + contract(act, w_down[...], 1, 0)


def first_half(bits, own_context, other_context, x, vectors, in_bias, w_out, w_in, w_down, parts):
    rows, width = x.shape
    local, hidden = own_context.shape[1], w_in.shape[1]
    tile = 256

    def row_block(columns):
        return pl.BlockSpec((tile, columns), lambda i, s: (i, 0))

    def whole(columns):
        return pl.BlockSpec((1, columns), lambda i, s: (0, 0))

    return pl.pallas_call(
        first_kernel,
        grid_spec=pltpu.PrefetchScalarGridSpec(
            num_scalar_prefetch=1,
            grid=(rows // tile,),
            in_specs=[row_block(local), row_block(local), row_block(width)]
            + [whole(width)] * 4
            + [whole(hidden)]
            + [ANYWHERE] * (3 + len(parts)),
            out_specs=[
                row_block(width),
                row_block(width),
                row_block(1),
                row_block(width),
                row_block(hidden),
                row_block(hidden),
            ],
            scratch_shapes=[
                pltpu.VMEM((local, width), LOW),
                pltpu.VMEM((local, width), LOW),
                pltpu.VMEM((width, hidden), LOW),
                pltpu.VMEM((hidden, width), LOW),
                pltpu.SemaphoreType.DMA((19,)),
            ],
        ),
        out_shape=[
            jax.ShapeDtypeStruct((rows, width), LOW),
            jax.ShapeDtypeStruct((rows, width), LOW),
            jax.ShapeDtypeStruct((rows, 1), WIDE),
            jax.ShapeDtypeStruct((rows, width), WIDE),
            jax.ShapeDtypeStruct((rows, hidden), LOW),
            jax.ShapeDtypeStruct((rows, hidden), LOW),
        ],
        cost_estimate=small_cost(),
        name="first_half",
    )(bits, own_context, other_context, x, *vectors, in_bias, w_out, w_in, w_down, *parts)


def second_kernel(
    bits_ref,
    hidden_ref,
    base_ref,
    cot_ref,
    slope_ref,
    normed_ref,
    scale_ref,
    gain_one_ref,
    gain_two_ref,
    shift_two_ref,
    in_bias_ref,
    w_out_ref,
    w_in_ref,
    w_down_ref,
    *refs,
):
    out_pieces, pieces = refs[:8], refs[8:16]
    output_ref, branch_ref, act_ref, own_grad_ref, other_grad_ref, attended_ref = refs[16:22]
    own_context_ref, other_context_ref, sums_ref, bias_sums_ref = refs[22:26]
    own_out, other_out, own_in, other_in, own_down, other_down, semaphores = refs[26:]
    rank = rank_of(bits_ref)
    loads = Loads(semaphores)
    other_in_ready = loads.group(in_parts(pieces, other_in, rank))
    other_down_ready = loads.group(down_parts(pieces, other_down, rank))
    own_down_ready = loads.group([(w_down_ref, own_down)])
    own_in_ready = loads.group([(w_in_ref, own_in)])
    out_ready = loads.group([(w_out_ref, own_out)] + out_parts(out_pieces, other_out, rank))
    loads.start()

    @pl.when(pl.program_id(0) == 0)
    def _():
        sums_ref[...] = jnp.zeros_like(sums_ref)
        bias_sums_ref[...] = jnp.zeros_like(bias_sums_ref)

    def count(ref, row, values):
        ref[row : row + 1] += jnp.sum(values, axis=0, keepdims=True)

    loads.wait(other_in_ready)
    act, slope = gelu_pair(contract(hidden_ref[...], other_in[...], 1, 0) + in_bias_ref[...])
    act = act.astype(LOW)
    act_ref[...] = act
    loads.wait(other_down_ready)
    pre_two = base_ref[...] + contract(act, other_down[...], 1, 0)
    normed, scale = normalize(pre_two)
    output_ref[...] = (normed * gain_two_ref[...] + shift_two_ref[...]).astype(LOW)
    cot = cot_ref[...].astype(WIDE)
    grad_pre_two = normalize_back(cot, normed, scale, gain_two_ref[...])
    count(sums_ref, 4, cot * normed)
    count(sums_ref, 5, cot)
    count(sums_ref, 3, grad_pre_two)
    branch_grad = grad_pre_two.astype(LOW)
    branch_ref[...] = branch_grad
    grad = contract(branch_grad, other_down[...], 1, 1) * slope
    count(bias_sums_ref, 1, grad)
    grad = grad.astype(LOW)
    other_grad_ref[...] = grad
    grad_hidden = grad_pre_two + contract(grad, other_in[...], 1, 1)
    loads.wait(own_down_ready)
    grad = contract(branch_grad, own_down[...], 1, 1) * slope_ref[...].astype(WIDE)
    count(bias_sums_ref, 0, grad)
    grad = grad.astype(LOW)
    own_grad_ref[...] = grad
    loads.wait(own_in_ready)
    grad_hidden += contract(grad, own_in[...], 1, 1)
    normed = normed_ref[...].astype(WIDE)
    grad_pre_one = normalize_back(grad_hidden, normed, scale_ref[...], gain_one_ref[...])
    count(sums_ref, 1, grad_hidden * normed)
    count(sums_ref, 2, grad_hidden)
    count(sums_ref, 0, grad_pre_one)
    attended = grad_pre_one.astype(LOW)
    attended_ref[...] = attended
    loads.wait(out_ready)
    own_context_ref[...] = contract(attended, own_out[...], 1, 1).astype(LOW)
    other_context_ref[...] = contract(attended, other_out[...], 1, 1).astype(LOW)


def second_half(bits, hidden_low, base, cot, slope, normed, scale, vectors, in_bias, w_out, w_in, w_down, out_pieces, pieces):
    rows, width = hidden_low.shape
    local, hidden = w_out.shape[0], w_in.shape[1]
    tile = 256

    def row_block(columns):
        return pl.BlockSpec((tile, columns), lambda i, s: (i, 0))

    def whole(columns, count=1):
        return pl.BlockSpec((count, columns), lambda i, s: (0, 0))

    def low(columns):
        return jax.ShapeDtypeStruct((rows, columns), LOW)

    return pl.pallas_call(
        second_kernel,
        grid_spec=pltpu.PrefetchScalarGridSpec(
            num_scalar_prefetch=1,
            grid=(rows // tile,),
            in_specs=[
                row_block(width),
                row_block(width),
                row_block(width),
                row_block(hidden),
                row_block(width),
                row_block(1),
            ]
            + [whole(width)] * 3
            + [whole(hidden)]
            + [ANYWHERE] * 19,
            out_specs=[
                row_block(width),
                row_block(width),
                row_block(hidden),
                row_block(hidden),
                row_block(hidden),
                row_block(width),
                row_block(local),
                row_block(local),
                whole(width, 8),
                whole(hidden, 8),
            ],
            scratch_shapes=[
                pltpu.VMEM((local, width), LOW),
                pltpu.VMEM((local, width), LOW),
                pltpu.VMEM((width, hidden), LOW),
                pltpu.VMEM((width, hidden), LOW),
                pltpu.VMEM((hidden, width), LOW),
                pltpu.VMEM((hidden, width), LOW),
                pltpu.SemaphoreType.DMA((43,)),
            ],
        ),
        out_shape=[
            low(width),
            low(width),
            low(hidden),
            low(hidden),
            low(hidden),
            low(width),
            low(local),
            low(local),
            jax.ShapeDtypeStruct((8, width), WIDE),
            jax.ShapeDtypeStruct((8, hidden), WIDE),
        ],
        cost_estimate=small_cost(),
        name="second_half",
    )(bits, hidden_low, base, cot, slope, normed, scale, *vectors, in_bias, w_out, w_in, w_down, *out_pieces, *pieces)


def down_kernel(bits_ref, act_ref, grad_ref, sent_ref, kept_ref):
    z = bits_ref[2]
    result = contract(act_ref[...], grad_ref[...], 0, 0)
    rows = result.shape[0] // 2

    def put(out_ref):
        for part in range(2):
            out_ref[0, part ^ z] = result[part * rows : (part + 1) * rows].astype(LOW)

    @pl.when(pl.program_id(0) < 2)
    def _():
        put(sent_ref)

    @pl.when(pl.program_id(0) >= 2)
    def _():
        put(kept_ref)


def down_pieces(bits, activated, grad):
    rows, hidden = activated.shape
    width = grad.shape[1]
    piece = (1, 2, hidden // 8, width)
    return pl.pallas_call(
        down_kernel,
        grid_spec=pltpu.PrefetchScalarGridSpec(
            num_scalar_prefetch=1,
            grid=(4,),
            in_specs=[
                pl.BlockSpec(
                    (rows, hidden // 4), lambda i, s: (0, (s[0] ^ (1 - i // 2)) * 2 + ((i % 2) ^ s[1]))
                ),
                pl.BlockSpec((rows, width), lambda i, s: (0, 0)),
            ],
            out_specs=[
                pl.BlockSpec(piece, lambda i, s: (jnp.minimum(i, 1), 0, 0, 0)),
                pl.BlockSpec(piece, lambda i, s: (jnp.maximum(i - 2, 0), 0, 0, 0)),
            ],
        ),
        out_shape=[jax.ShapeDtypeStruct((2,) + piece[1:], LOW)] * 2,
        cost_estimate=small_cost(),
        name="down_pieces",
    )(bits, activated, grad)


def in_kernel(bits_ref, hidden_ref, grad_ref, sent_ref, kept_ref):
    x, z = bits_ref[1], bits_ref[2]
    result = contract(hidden_ref[...], grad_ref[...], 0, 0)
    rows, columns = result.shape[0] // 2, result.shape[1] // 2

    def put(out_ref):
        for side in range(2):
            for part in range(2):
                out_ref[side ^ x, part ^ z] = result[
                    part * rows : (part + 1) * rows, side * columns : (side + 1) * columns
                ].astype(LOW)

    @pl.when(pl.program_id(0) == 0)
    def _():
        put(sent_ref)

    @pl.when(pl.program_id(0) == 1)
    def _():
        put(kept_ref)


def in_pieces(bits, hidden_low, grad):
    rows, width = hidden_low.shape
    hidden = grad.shape[1]
    piece = (2, 2, width // 2, hidden // 4)
    return pl.pallas_call(
        in_kernel,
        grid_spec=pltpu.PrefetchScalarGridSpec(
            num_scalar_prefetch=1,
            grid=(2,),
            in_specs=[
                pl.BlockSpec((rows, width), lambda i, s: (0, 0)),
                pl.BlockSpec((rows, hidden // 2), lambda i, s: (0, s[0] ^ (1 - i))),
            ],
            out_specs=[pl.BlockSpec(piece, lambda i, s: (0, 0, 0, 0))] * 2,
        ),
        out_shape=[jax.ShapeDtypeStruct(piece, LOW)] * 2,
        cost_estimate=small_cost(),
        name="in_pieces",
    )(bits, hidden_low, grad)


def heads_kernel(bits_ref, x_ref, grads_ref, context_ref, attended_ref, sent_ref, kept_ref, scratch):
    core = bits_ref[0]
    mine = bits_ref[1] * 2 + bits_ref[2]
    extent, local = scratch.shape[1:]

    @pl.when(pl.program_id(0) < 3)
    def _():
        result = contract(x_ref[...], grads_ref[0], 0, 0)
        for part in range(8):
            scratch[part] = result[part * extent : (part + 1) * extent]

    @pl.when(pl.program_id(0) == 3)
    def _():
        result = contract(context_ref[...], attended_ref[...], 0, 0)
        for part in range(8):
            rows, side = part % 4, part // 4
            scratch[part] = result[rows * extent : (rows + 1) * extent, side * local : (side + 1) * local]

    for part in range(4):
        sent_ref[part ^ mine, 0] = scratch[(1 - core) * 4 + part].astype(LOW)
        kept_ref[part ^ mine, 0] = scratch[core * 4 + part].astype(LOW)


def heads_pieces(bits, tokens, grads, context, attended):
    rows, width = tokens.shape
    local = context.shape[1]
    return pl.pallas_call(
        heads_kernel,
        grid_spec=pltpu.PrefetchScalarGridSpec(
            num_scalar_prefetch=1,
            grid=(4,),
            in_specs=[
                pl.BlockSpec((rows, width), lambda j, s: (0, 0)),
                pl.BlockSpec((1, rows, local), lambda j, s: (jnp.minimum(j, 2), 0, 0)),
                pl.BlockSpec((rows, local), lambda j, s: (0, 0)),
                pl.BlockSpec((rows, width), lambda j, s: (0, 0)),
            ],
            out_specs=[pl.BlockSpec((4, 1, width // 8, local), lambda j, s: (0, j, 0, 0))] * 2,
            scratch_shapes=[pltpu.VMEM((8, width // 8, local), WIDE)],
        ),
        out_shape=[jax.ShapeDtypeStruct((4, 4, width // 8, local), LOW)] * 2,
        cost_estimate=small_cost(),
        name="heads_pieces",
    )(bits, tokens, grads, context, attended)


def add(*arrays):
    total = arrays[0].astype(WIDE)
    for array in arrays[1:]:
        total = total + array.astype(WIDE)
    return total.astype(LOW)


class Chain:
    AXES = {"x": 1, "z": 2}

    def __init__(self, order, size):
        self.order, self.size = order, size
        self.terms = {"own": [], "other": []}

    def begin(self, side, sent, kept):
        for array in (kept, swap(sent, 0, self.size)):
            self.terms[side].append((array, (), ("x", "z")))

    def summed(self, terms):
        def cut(*arrays):
            parts = []
            for array, (_, picks, _) in zip(arrays, terms):
                for axis, index in picks:
                    array = lax.index_in_dim(array, index, axis, False)
                parts.append(array)
            return add(*parts)

        return self.order.run(cut, *[array for array, _, _ in terms])

    def halve(self, side, name):
        def pick(term, index):
            array, picks, axes = term
            if name not in axes:
                return term
            left = tuple(axis for axis in axes if axis != name)
            return array, picks + ((axes.index(name), index),), left

        terms = self.terms[side]
        there = [pick(term, 1) for term in terms if name in term[2]]
        arrived = swap(self.summed(there), self.AXES[name], self.size)
        self.terms[side] = [pick(term, 0) for term in terms] + [(arrived, (), there[0][2])]

    def cross(self):
        terms = self.terms["other"]
        self.terms["own"].append((across(self.summed(terms)), (), terms[0][2]))

    def total(self):
        self.kept = self.summed(self.terms["own"])

    def exchange(self, bit):
        self.terms["own"] = [(array, (), ()) for array in (self.kept, swap(self.kept, bit, self.size))]

    def spread(self):
        self.pieces = [self.kept] + [swap(self.kept, bit, self.size) for bit in (2, 1, 0)]

    def spread_on(self):
        kept, z, x, partner = self.pieces
        (z,) = self.order.sync(z)
        self.pieces = [kept, z, x, swap(z, 1, self.size), partner, swap(z, 0, self.size)]

    def finish(self):
        kept, z, x, xz, partner, partner_z = self.pieces
        x, xz = self.order.sync(x, xz)
        return [kept, z, x, xz, partner, partner_z, swap(x, 0, self.size), swap(xz, 0, self.size)]


def widen_kernel(bits_ref, *refs):
    for index in range(8):

        @pl.when(pl.program_id(0) == index)
        def _():
            refs[-1][...] = refs[index][...].astype(WIDE)


def widen(bits, pieces, shape, block, place):
    def out_place(r, s):
        q = r ^ (s[0] * 4 + s[1] * 2 + s[2])
        return place(q // 4, (q // 2) % 2, q % 2)

    piece = pieces[0].shape
    return pl.pallas_call(
        widen_kernel,
        grid_spec=pltpu.PrefetchScalarGridSpec(
            num_scalar_prefetch=1,
            grid=(8,),
            in_specs=[pl.BlockSpec(piece, lambda r, s: (0,) * len(piece))] * 8,
            out_specs=pl.BlockSpec(block, out_place),
        ),
        out_shape=jax.ShapeDtypeStruct(shape, WIDE),
        name="widen",
    )(bits, *pieces)


def widen_heads_kernel(bits_ref, *refs):
    for index in range(8):

        @pl.when(pl.program_id(0) == index)
        def _():
            refs[-2][...] = refs[index][:3].astype(WIDE)
            refs[-1][...] = refs[index][3].astype(WIDE)


def widen_heads(bits, pieces, width, local):
    def bits_of(r, s):
        q = r ^ (s[0] * 4 + s[1] * 2 + s[2])
        return q // 4, q % 4

    piece = pieces[0].shape
    return pl.pallas_call(
        widen_heads_kernel,
        grid_spec=pltpu.PrefetchScalarGridSpec(
            num_scalar_prefetch=1,
            grid=(8,),
            in_specs=[pl.BlockSpec(piece, lambda r, s: (0,) * len(piece))] * 8,
            out_specs=[
                pl.BlockSpec((3,) + piece[1:], lambda r, s: (0, bits_of(r, s)[0] * 4 + bits_of(r, s)[1], 0)),
                pl.BlockSpec(piece[1:], lambda r, s: (bits_of(r, s)[1], bits_of(r, s)[0])),
            ],
        ),
        out_shape=[
            jax.ShapeDtypeStruct((3, width, local), WIDE),
            jax.ShapeDtypeStruct((local, width), WIDE),
        ],
        name="widen_heads",
    )(bits, *pieces)


def body(
    tokens,
    lengths,
    w_qkv,
    q_bias,
    v_bias,
    w_out,
    out_bias,
    gain_one,
    shift_one,
    w_in,
    in_bias,
    w_down,
    down_bias,
    gain_two,
    shift_two,
    cotangent,
):
    rows, width = cotangent.shape
    seq_len = tokens.shape[0] // lengths.shape[0]
    sequences = rows // seq_len
    local = w_qkv.shape[2]
    hidden = w_in.shape[1]
    size = lax.axis_size("dp")
    pair = lax.axis_index("tensor")
    dp = lax.axis_index("dp")
    bits = jnp.stack(halves(dp)).astype(jnp.int32)
    rank = (dp & 1) * 4 + ((dp >> 1) & 1) * 2 + ((dp >> 2) & 1)

    def row(vector):
        return vector.reshape(1, -1)

    def eighth(array, axis):
        extent = array.shape[axis] // 8
        return lax.dynamic_slice_in_dim(array, rank * extent, extent, axis)

    def stacked(array):
        columns = array.shape[1] // 2
        return jnp.concatenate([array[:, :columns], array[:, columns:]], axis=0)

    qkv_own = jnp.transpose(w_qkv, (1, 0, 2))
    attention_piece = jnp.concatenate(
        [eighth(qkv_own, 1), stacked(eighth(w_out, 0))[None]], axis=0
    )
    forward_piece = jnp.concatenate([stacked(eighth(w_in, 0)), eighth(w_down, 0)], axis=0)
    order = Order(attention_piece)
    attention_fetch = Fetch(order, attention_piece, size)
    biases = jnp.concatenate([q_bias, v_bias, in_bias])
    (biases,) = order.sync(biases)
    biases_other = across(biases)
    (forward_piece,) = order.sync(forward_piece)
    forward_fetch = Fetch(order, forward_piece, size)

    x = lax.dynamic_slice_in_dim(tokens, pair * rows, rows, 0)
    own_lengths = lax.dynamic_slice_in_dim(lengths, pair * sequences, sequences, 0)

    q_own, k_own, v_own = order.run(
        lambda x: project(bits, x, 0, rows, local, row(biases[: 2 * local]), [qkv_own]), x
    )
    attention_fetch.pass_on()
    begun = order.run(lambda *qkv: attend(own_lengths, *qkv, 0), q_own, k_own, v_own)
    attention_pieces = attention_fetch.finish()
    for sequence in range(1, sequences):
        begun = order.run(
            lambda *args: attend(own_lengths, *args[:3], sequence, *args[3:]), q_own, k_own, v_own, *begun
        )
    context_own, probs_own = begun
    forward_fetch.pass_on()
    q_other, k_other, v_other = order.run(
        lambda *parts: project(bits, x, 0, rows, local, row(biases_other[: 2 * local]), parts),
        *attention_pieces,
    )
    begun = order.run(lambda *qkv: attend(own_lengths, *qkv, 0), q_other, k_other, v_other)
    forward_pieces = forward_fetch.finish()
    for sequence in range(1, sequences):
        begun = order.run(
            lambda *args: attend(own_lengths, *args[:3], sequence, *args[3:]),
            q_other, k_other, v_other, *begun,
        )
    context_other, probs_other = begun

    hidden_low, normed_one, scale_one, base, act_own, slope_own = order.run(
        lambda context_own, context_other: first_half(
            bits,
            context_own,
            context_other,
            x,
            [row(out_bias), row(gain_one), row(shift_one), row(down_bias)],
            row(in_bias),
            w_out,
            w_in,
            w_down,
            attention_pieces,
        ),
        context_own,
        context_other,
    )
    (
        output,
        branch_grad,
        act_other,
        grad_own,
        grad_other,
        attended_grad,
        context_grad_own,
        context_grad_other,
        sums,
        bias_sums,
    ) = order.run(
        lambda hidden_low, *pieces: second_half(
            bits,
            hidden_low,
            base,
            cotangent,
            slope_own,
            normed_one,
            scale_one,
            [row(gain_one), row(gain_two), row(shift_two)],
            row(biases_other[2 * local :]),
            w_out,
            w_in,
            w_down,
            attention_pieces,
            pieces,
        ),
        hidden_low,
        *forward_pieces,
    )

    down, entry, heads = Chain(order, size), Chain(order, size), Chain(order, size)
    extra = range(3, size.bit_length() - 1)

    def down_grad(act):
        return order.run(lambda act: down_pieces(bits, act, branch_grad), act)

    def in_grad(grad):
        return order.run(lambda grad: in_pieces(bits, hidden_low, grad), grad)

    def heads_back(q, k, v, context, context_grad, probs):
        return order.run(
            lambda *args: attend_back(*args, sequences), q, k, v, context, context_grad, probs
        )

    def heads_grad(grads, context):
        pieces = order.run(lambda grads: heads_pieces(bits, x, grads, context, attended_grad), grads)
        return [piece.reshape(2, 2, *piece.shape[1:]) for piece in pieces]

    down.begin("other", *down_grad(act_other))
    entry.begin("other", *in_grad(grad_other))
    down.cross()
    entry.begin("own", *in_grad(grad_own))
    entry.halve("other", "x")
    down.begin("own", *down_grad(act_own))
    project_other = heads_back(
        q_other, k_other, v_other, context_other, context_grad_other, probs_other
    )
    entry.halve("other", "z")
    entry.halve("own", "x")
    down.halve("own", "x")
    heads.begin("other", *heads_grad(project_other, context_other))
    entry.cross()
    project_own = heads_back(q_own, k_own, v_own, context_own, context_grad_own, probs_own)
    entry.halve("own", "z")
    down.halve("own", "z")
    heads.halve("other", "x")
    heads.begin("own", *heads_grad(project_own, context_own))
    entry.total()
    down.total()
    for bit in extra:
        entry.exchange(bit)
        down.exchange(bit)
        heads_step = bit == 3
        if heads_step:
            heads.halve("other", "z")
            heads.halve("own", "x")
            input_grad = order.run(
                lambda *grads: project_back(bits, *grads, attended_grad, qkv_own, attention_pieces),
                project_own,
                project_other,
            )
            heads.cross()
        entry.total()
        down.total()
    entry.spread()
    down.spread()

    def head_sums(grads):
        return jnp.concatenate(
            [jnp.sum(grads[0].astype(WIDE), axis=0), jnp.sum(grads[2].astype(WIDE), axis=0)]
        )

    shared = sums[:6].reshape(-1)
    own_sums, other_sums, shared = order.run(
        lambda own, other, shared: (
            jnp.concatenate([head_sums(own), bias_sums[0]]),
            jnp.concatenate([shared, head_sums(other), bias_sums[1]]),
            shared,
        ),
        project_own,
        project_other,
        shared,
    )
    arrived = across(other_sums)
    heads.halve("own", "z")
    entry.spread_on()
    down.spread_on()
    vectors = order.run(
        lambda own, shared, arrived: jnp.concatenate([shared, own]) + arrived, own_sums, shared, arrived
    )
    heads.total()
    for bit in extra:
        heads.exchange(bit)
        arrived = swap(vectors, bit, size)
        if bit == 3:
            in_parts_all = entry.finish()
            down_parts_all = down.finish()
        vectors = order.run(jnp.add, vectors, arrived)
        if bit == 3:
            arrived = swap(vectors, 0, size)
            grad_w_in = order.run(
                lambda *pieces: widen(
                    bits, pieces, (width, hidden), pieces[0].shape, lambda c, i, z: (z, c * 2 + i)
                ),
                *in_parts_all,
            )
            vectors = order.run(jnp.add, vectors, arrived)
        heads.total()
    heads.spread()
    arrived = swap(vectors, 1, size)
    grad_w_down = order.run(
        lambda *pieces: widen(
            bits, pieces, (hidden, width), pieces[0].shape, lambda c, i, z: (c * 4 + i * 2 + z, 0)
        ),
        *down_parts_all,
    )
    vectors = order.run(jnp.add, vectors, arrived)
    heads.spread_on()
    arrived = swap(vectors, 2, size)
    vectors = order.run(jnp.add, vectors, arrived)
    count = 6 * width
    shared, head_biases, grad_in_bias = (
        vectors[:count].reshape(6, width),
        vectors[count : count + 2 * local],
        vectors[count + 2 * local :],
    )
    grad_qkv, grad_w_out = order.run(
        lambda *pieces: widen_heads(bits, pieces, width, local), *heads.finish()
    )

    return (
        output,
        input_grad,
        jnp.transpose(grad_qkv, (1, 0, 2)),
        head_biases[:local],
        head_biases[local:],
        grad_w_out,
        shared[0],
        shared[1],
        shared[2],
        grad_w_in,
        grad_in_bias,
        grad_w_down,
        shared[3],
        shared[4],
        shared[5],
    )


def solution(mesh):
    placed = (
        P("dp", None),
        P("dp"),
        P(None, None, "tensor"),
        P("tensor"),
        P("tensor"),
        P("tensor", None),
        P(),
        P(),
        P(),
        P(None, "tensor"),
        P("tensor"),
        P("tensor", None),
        P(),
        P(),
        P(),
        P(("dp", "tensor"), None),
    )
    return jax.shard_map(
        body,
        mesh=mesh,
        in_specs=placed,
        out_specs=(
            P(("dp", "tensor"), None),
            P(("dp", "tensor"), None),
            P(None, None, "tensor"),
            P("tensor"),
            P("tensor"),
            P("tensor", None),
            P(),
            P(),
            P(),
            P(None, "tensor"),
            P("tensor"),
            P("tensor", None),
            P(),
            P(),
            P(),
        ),
        check_vma=False,
    )
```

```python
import jax
import jax.numpy as jnp
from jax import lax
from jax.experimental import pallas as pl
from jax.experimental.pallas import tpu as pltpu
from jax.sharding import PartitionSpec as P

HEAD_DIM = 64
EPSILON = 1e-06
MASKED = -1000000000.0
LOW = jnp.bfloat16
WIDE = jnp.float32
RSQRT2PI = 0.3989422804014327


def contract(a, b, dim_a, dim_b):
    return lax.dot_general(
        a, b, (((dim_a,), (dim_b,)), ((), ())), preferred_element_type=WIDE
    )


def swap(array, bit, size):
    return lax.ppermute(array, "dp", [(i, i ^ (1 << bit)) for i in range(size)])


def across(array):
    return lax.ppermute(array, "tensor", [(0, 1), (1, 0)])


ANYWHERE = pl.BlockSpec(memory_space=pl.ANY)


def small_cost(flops=10**6):
    return pl.CostEstimate(flops=flops, bytes_accessed=10**5, transcendentals=0)


def attend_kernel(bits_ref, length_ref, q_ref, k_ref, v_ref, context_ref, probs_ref):
    length = length_ref[bits_ref[3] * pl.num_programs(0) + pl.program_id(0)]
    rows = q_ref.shape[0]
    lane = lax.broadcasted_iota(jnp.int32, (rows, 128), 1)
    slot = lax.broadcasted_iota(jnp.int32, (rows, 128), 0)
    masked = jnp.where(slot < length, 0.0, MASKED).astype(LOW)
    q, k, v = q_ref[...], k_ref[...], v_ref[...]
    zero, one = jnp.zeros_like(q), jnp.ones_like(q)
    contexts = []
    for head in range(2):
        mine = (lane >= 64) if head else (lane < 64)
        mark = lane == (0 if head else 64)
        k_head = jnp.where(mine, k, jnp.where(mark, masked, zero))
        q_head = jnp.where(mine, q, jnp.where(mark, one, zero))
        scores = contract(k_head, q_head, 1, 1)
        top = jnp.max(scores, axis=0, keepdims=True)
        exponent = jnp.exp(scores - top)
        total = jnp.sum(exponent, axis=0, keepdims=True)
        probs = (exponent * (1.0 / total)).astype(LOW)
        probs_ref[head] = probs
        contexts.append(contract(probs, v, 0, 0))
    context_ref[...] = jnp.where(lane < 64, contexts[0], contexts[1]).astype(LOW)


def attend(bits, lengths, q, k, v):
    rows, width = q.shape
    sequences = lengths.shape[0] // 2
    length, pairs = rows // sequences, width // 128
    block = pl.BlockSpec((length, 128), lambda s, h, *_: (s, h))
    return pl.pallas_call(
        attend_kernel,
        grid_spec=pltpu.PrefetchScalarGridSpec(
            num_scalar_prefetch=2,
            grid=(sequences, pairs),
            in_specs=[block] * 3,
            out_specs=[
                block,
                pl.BlockSpec((2, length, length), lambda s, h, *_: (s * pairs + h, 0, 0)),
            ],
        ),
        out_shape=[
            jax.ShapeDtypeStruct((rows, width), LOW),
            jax.ShapeDtypeStruct((sequences * pairs * 2, length, length), LOW),
        ],
        cost_estimate=small_cost(),
        name="attend",
    )(bits, lengths, q, k, v)


def attend_back_kernel(q_ref, k_ref, v_ref, context_ref, grad_ref, probs_ref, out_ref):
    rows = q_ref.shape[0]
    lane = lax.broadcasted_iota(jnp.int32, (rows, 128), 1)
    q, k, v, grad = q_ref[...], k_ref[...], v_ref[...], grad_ref[...]
    inner = pltpu.roll(grad.astype(WIDE) * context_ref[...].astype(WIDE), 64, 1).astype(LOW)
    zero, minus = jnp.zeros_like(q), -jnp.ones_like(q)
    grad_q = grad_k = grad_v = 0.0
    for head in range(2):
        mine = (lane >= 64) if head else (lane < 64)
        centred = contract(jnp.where(mine, v, minus), jnp.where(mine, grad, inner), 1, 1)
        probs = probs_ref[head]
        grad_scores = (probs.astype(WIDE) * centred).astype(LOW)
        grad_v += contract(probs, jnp.where(mine, grad, zero), 1, 0)
        grad_k += contract(grad_scores, jnp.where(mine, q, zero), 1, 0)
        grad_q += contract(grad_scores, jnp.where(mine, k, zero), 0, 0)
    out_ref[0] = (grad_q * HEAD_DIM**-0.5).astype(LOW)
    out_ref[1] = grad_k.astype(LOW)
    out_ref[2] = grad_v.astype(LOW)


def attend_back(q, k, v, context, grad, probs, sequences):
    rows, width = q.shape
    length, pairs = rows // sequences, width // 128
    block = pl.BlockSpec((length, 128), lambda s, h: (s, h))
    return pl.pallas_call(
        attend_back_kernel,
        grid=(sequences, pairs),
        in_specs=[block] * 5
        + [pl.BlockSpec((2, length, length), lambda s, h: (s * pairs + h, 0, 0))],
        out_specs=pl.BlockSpec((3, length, 128), lambda s, h: (0, s, h)),
        out_shape=jax.ShapeDtypeStruct((3, rows, width), LOW),
        cost_estimate=small_cost(),
        name="attend_back",
    )(q, k, v, context, grad, probs)


def pack_kernel(bits_ref, qkv_ref, out_ref, in_ref, down_ref, attention_ref, forward_ref):
    attention_ref[:3] = qkv_ref[...]
    for target, source in ((attention_ref.at[3], out_ref), (forward_ref, in_ref)):
        rows, width = source.shape[0], source.shape[1] // 2
        for side in range(2):
            target[side * rows : (side + 1) * rows] = source[:, side * width : (side + 1) * width]
    rows = down_ref.shape[0]
    forward_ref[rows:] = down_ref[...]


def pack(bits, w_qkv, w_out, w_in, w_down):
    quarters = [(3, w_qkv.shape[1] // 4, w_qkv.shape[2])]
    quarters += [(w.shape[0] // 4, w.shape[1]) for w in (w_out, w_in, w_down)]
    _, rows, local = quarters[0]
    attention, forward = (4, rows, local), (2 * quarters[3][0], quarters[3][1])

    def place(*index):
        return lambda i, s: tuple(s[0] * 2 + s[1] if k else 0 for k in index)

    return pl.pallas_call(
        pack_kernel,
        grid_spec=pltpu.PrefetchScalarGridSpec(
            num_scalar_prefetch=1,
            grid=(1,),
            in_specs=[pl.BlockSpec(quarters[0], place(0, 1, 0))]
            + [pl.BlockSpec(quarter, place(1, 0)) for quarter in quarters[1:]],
            out_specs=[pl.BlockSpec(attention, place(0, 0, 0)), pl.BlockSpec(forward, place(0, 0))],
        ),
        out_shape=[jax.ShapeDtypeStruct(attention, LOW), jax.ShapeDtypeStruct(forward, LOW)],
        cost_estimate=small_cost(),
        name="pack",
    )(bits, w_qkv, w_out, w_in, w_down)


class Order:
    def __init__(self, first):
        self.last = first

    def sync(self, *arrays):
        arrays, self.last = lax.optimization_barrier((arrays, self.last))
        return arrays

    def run(self, step, *arrays):
        arrays = self.sync(*arrays)
        result = step(*arrays)
        self.last = result[0] if isinstance(result, (list, tuple)) else result
        return result


class Fetch:
    def __init__(self, order, piece, size):
        self.order, self.size = order, size
        self.here = across(piece)

    def pass_on(self):
        (self.here,) = self.order.sync(self.here)
        self.x = swap(self.here, 1, self.size)
        self.partner = swap(self.here, 0, self.size)

    def finish(self):
        (self.x,) = self.order.sync(self.x)
        return [self.here, self.x, self.partner, swap(self.x, 0, self.size)]


def rank_of(bits_ref):
    return bits_ref[0] * 2 + bits_ref[1]


class Loads:
    def __init__(self, semaphores):
        self.semaphores, self.count, self.groups = semaphores, 0, []

    def group(self, pairs):
        copies = []
        for source, target in pairs:
            copies.append(pltpu.make_async_copy(source, target, self.semaphores.at[self.count]))
            self.count += 1
        self.groups.append(copies)
        return len(self.groups) - 1

    def start(self):
        @pl.when(pl.program_id(0) == 0)
        def _():
            for copies in self.groups:
                for copy in copies:
                    copy.start()

    def wait(self, group):
        @pl.when(pl.program_id(0) == 0)
        def _():
            for copy in self.groups[group]:
                copy.wait()


def qkv_parts(parts, target, rank):
    extent = target.shape[1] // 4
    return [
        (part.at[:3], target.at[:, pl.ds(pl.multiple_of((r ^ rank) * extent, 16), extent)])
        for r, part in enumerate(parts)
    ]


def out_parts(parts, target, rank):
    extent, width = target.shape[0] // 4, target.shape[1] // 2
    return [
        (
            part.at[3, pl.ds(side * extent, extent)],
            target.at[pl.ds(pl.multiple_of((r ^ rank) * extent, 16), extent), pl.ds(side * width, width)],
        )
        for r, part in enumerate(parts)
        for side in range(2)
    ]


def in_parts(parts, target, rank):
    extent, width = target.shape[0] // 4, target.shape[1] // 2
    return [
        (
            part.at[pl.ds(side * extent, extent)],
            target.at[pl.ds(pl.multiple_of((r ^ rank) * extent, 16), extent), pl.ds(side * width, width)],
        )
        for r, part in enumerate(parts)
        for side in range(2)
    ]


def down_parts(parts, target, rank):
    extent = target.shape[0] // 4
    return [
        (part.at[pl.ds(extent, extent)], target.at[pl.ds(pl.multiple_of((r ^ rank) * extent, 16), extent)])
        for r, part in enumerate(parts)
    ]


def project_kernel(bits_ref, x_ref, biases_ref, *refs):
    parts, (q_ref, k_ref, v_ref, weights, semaphores) = refs[:-5], refs[-5:]
    loads = Loads(semaphores)
    if len(parts) == 1:
        ready = loads.group([(parts[0], weights)])
    else:
        ready = loads.group(qkv_parts(parts, weights, rank_of(bits_ref)))
    loads.start()
    loads.wait(ready)
    x = x_ref[...]
    queries = (contract(x, weights[0], 1, 0) + biases_ref[0:1]).astype(LOW)
    q_ref[...] = queries * HEAD_DIM**-0.5
    k_ref[...] = contract(x, weights[1], 1, 0).astype(LOW)
    v_ref[...] = (contract(x, weights[2], 1, 0) + biases_ref[1:2]).astype(LOW)


def project(bits, tokens, biases, parts):
    rows, width = tokens.shape[0] // 2, tokens.shape[1]
    local = biases.shape[1]
    tile = 512
    steps = rows // tile
    return pl.pallas_call(
        project_kernel,
        grid_spec=pltpu.PrefetchScalarGridSpec(
            num_scalar_prefetch=1,
            grid=(steps,),
            in_specs=[
                pl.BlockSpec((tile, width), lambda i, s: (s[3] * steps + i, 0)),
                pl.BlockSpec(biases.shape, lambda i, s: (0, 0)),
            ]
            + [ANYWHERE] * len(parts),
            out_specs=[pl.BlockSpec((tile, local), lambda i, s: (i, 0))] * 3,
            scratch_shapes=[pltpu.VMEM((3, width, local), LOW), pltpu.SemaphoreType.DMA((4,))],
        ),
        out_shape=[jax.ShapeDtypeStruct((rows, local), LOW)] * 3,
        cost_estimate=small_cost(),
        name="project",
    )(bits, tokens, biases, *parts)


def project_back_kernel(bits_ref, own_ref, other_ref, grad_ref, weights_ref, *refs):
    parts, (out_ref, own_weights, other_weights, semaphores) = refs[:-4], refs[-4:]
    loads = Loads(semaphores)
    own_ready = loads.group([(weights_ref, own_weights)])
    other_ready = loads.group(qkv_parts(parts, other_weights, rank_of(bits_ref)))
    loads.start()
    loads.wait(own_ready)
    total = grad_ref[...].astype(WIDE)
    for index in range(3):
        total += contract(own_ref[index], own_weights[index], 1, 1)
    loads.wait(other_ready)
    for index in range(3):
        total += contract(other_ref[index], other_weights[index], 1, 1)
    out_ref[...] = total.astype(LOW)


def project_back(bits, own, other, grad, weights, parts):
    rows, width = grad.shape
    local = own.shape[2]
    tile = 256
    block = pl.BlockSpec((3, tile, local), lambda i, s: (0, i, 0))
    row_block = pl.BlockSpec((tile, width), lambda i, s: (i, 0))
    return pl.pallas_call(
        project_back_kernel,
        grid_spec=pltpu.PrefetchScalarGridSpec(
            num_scalar_prefetch=1,
            grid=(rows // tile,),
            in_specs=[block, block, row_block] + [ANYWHERE] * (1 + len(parts)),
            out_specs=row_block,
            scratch_shapes=[pltpu.VMEM((3, width, local), LOW)] * 2 + [pltpu.SemaphoreType.DMA((5,))],
        ),
        out_shape=jax.ShapeDtypeStruct((rows, width), LOW),
        cost_estimate=small_cost(),
        name="project_back",
    )(bits, own, other, grad, weights, *parts)


def normalize(values):
    average = jnp.mean(values, axis=-1, keepdims=True)
    centred = values - average
    scale = lax.rsqrt(jnp.mean(centred * centred, axis=-1, keepdims=True) + EPSILON)
    return centred * scale, scale


def normalize_back(grad, normed, scale, gain):
    grad_normed = grad * gain
    first = jnp.mean(grad_normed, axis=-1, keepdims=True)
    second = jnp.mean(grad_normed * normed, axis=-1, keepdims=True)
    return scale * (grad_normed - first - normed * second)


TAIL = (
    0.0356748104095459,
    -0.15720322728157043,
    0.20635373890399933,
    -0.053683843463659286,
    0.12856172025203705,
    0.09991346299648285,
    0.12075395882129669,
    0.11962930113077164,
)


def gelu_pair(values):
    t = 1.0 / (1.0 + 0.3 * jnp.abs(values))
    bell = jnp.exp(-0.5 * (values * values))
    series = TAIL[0]
    for coefficient in TAIL[1:]:
        series = series * t + coefficient
    tail = bell * (t * series)
    below = jnp.where(values < 0.0, tail, 1.0 - tail)
    return values * below, below + RSQRT2PI * (values * bell)


def in_bias_of(biases_ref):
    return jnp.concatenate([biases_ref[i : i + 1] for i in range(2, biases_ref.shape[0])], axis=1)


def first_kernel(
    bits_ref,
    own_context_ref,
    other_context_ref,
    x_ref,
    vectors_ref,
    biases_ref,
    w_out_ref,
    w_in_ref,
    w_down_ref,
    *refs,
):
    parts = refs[:4]
    hidden_ref, normed_ref, scale_ref, base_ref, act_ref, slope_ref = refs[4:10]
    own_out, other_out, w_in, w_down, semaphores = refs[10:]
    out_bias, gain, shift, down_bias = [vectors_ref[i : i + 1] for i in range(4)]
    loads = Loads(semaphores)
    out_ready = loads.group([(w_out_ref, own_out)] + out_parts(parts, other_out, rank_of(bits_ref)))
    in_ready = loads.group([(w_in_ref, w_in)])
    down_ready = loads.group([(w_down_ref, w_down)])
    loads.start()
    loads.wait(out_ready)
    pre_one = contract(own_context_ref[...], own_out[...], 1, 0)
    pre_one += contract(other_context_ref[...], other_out[...], 1, 0)
    pre_one += out_bias + x_ref[...].astype(WIDE)
    normed, scale = normalize(pre_one)
    hidden = normed * gain + shift
    hidden_low = hidden.astype(LOW)
    hidden_ref[...] = hidden_low
    normed_ref[...] = normed.astype(LOW)
    scale_ref[...] = scale
    loads.wait(in_ready)
    act, slope = gelu_pair(contract(hidden_low, w_in[...], 1, 0) + in_bias_of(biases_ref))
    act = act.astype(LOW)
    act_ref[...] = act
    slope_ref[...] = slope.astype(LOW)
    loads.wait(down_ready)
    base_ref[...] = hidden + down_bias + contract(act, w_down[...], 1, 0)


def first_half(bits, own_context, other_context, tokens, vectors, biases, w_out, w_in, w_down, parts):
    rows, local = own_context.shape
    width, hidden = w_in.shape
    tile = 256
    steps = rows // tile

    def row_block(columns):
        return pl.BlockSpec((tile, columns), lambda i, s: (i, 0))

    def whole(array):
        return pl.BlockSpec(array.shape, lambda i, s: (0, 0))

    return pl.pallas_call(
        first_kernel,
        grid_spec=pltpu.PrefetchScalarGridSpec(
            num_scalar_prefetch=1,
            grid=(rows // tile,),
            in_specs=[row_block(local), row_block(local)]
            + [pl.BlockSpec((tile, width), lambda i, s: (s[3] * steps + i, 0))]
            + [whole(vectors), whole(biases)]
            + [ANYWHERE] * (3 + len(parts)),
            out_specs=[
                row_block(width),
                row_block(width),
                row_block(1),
                row_block(width),
                row_block(hidden),
                row_block(hidden),
            ],
            scratch_shapes=[
                pltpu.VMEM((local, width), LOW),
                pltpu.VMEM((local, width), LOW),
                pltpu.VMEM((width, hidden), LOW),
                pltpu.VMEM((hidden, width), LOW),
                pltpu.SemaphoreType.DMA((11,)),
            ],
        ),
        out_shape=[
            jax.ShapeDtypeStruct((rows, width), LOW),
            jax.ShapeDtypeStruct((rows, width), LOW),
            jax.ShapeDtypeStruct((rows, 1), WIDE),
            jax.ShapeDtypeStruct((rows, width), WIDE),
            jax.ShapeDtypeStruct((rows, hidden), LOW),
            jax.ShapeDtypeStruct((rows, hidden), LOW),
        ],
        cost_estimate=small_cost(),
        name="first_half",
    )(bits, own_context, other_context, tokens, vectors, biases, w_out, w_in, w_down, *parts)


def second_kernel(
    bits_ref,
    hidden_ref,
    base_ref,
    cot_ref,
    slope_ref,
    normed_ref,
    scale_ref,
    vectors_ref,
    biases_ref,
    w_out_ref,
    w_in_ref,
    w_down_ref,
    *refs,
):
    out_pieces, pieces = refs[:4], refs[4:8]
    output_ref, branch_ref, act_ref, own_grad_ref, other_grad_ref, attended_ref = refs[8:14]
    own_context_ref, other_context_ref, sums_ref, bias_sums_ref = refs[14:18]
    own_out, other_out, own_in, other_in, own_down, other_down, semaphores = refs[18:]
    gain_one, gain_two, shift_two = vectors_ref[1:2], vectors_ref[4:5], vectors_ref[5:6]
    rank = rank_of(bits_ref)
    loads = Loads(semaphores)
    other_in_ready = loads.group(in_parts(pieces, other_in, rank))
    other_down_ready = loads.group(down_parts(pieces, other_down, rank))
    own_down_ready = loads.group([(w_down_ref, own_down)])
    own_in_ready = loads.group([(w_in_ref, own_in)])
    out_ready = loads.group([(w_out_ref, own_out)] + out_parts(out_pieces, other_out, rank))
    loads.start()

    @pl.when(pl.program_id(0) == 0)
    def _():
        sums_ref[...] = jnp.zeros_like(sums_ref)
        bias_sums_ref[...] = jnp.zeros_like(bias_sums_ref)

    def count(ref, row, values):
        ref[row : row + 1] += jnp.sum(values, axis=0, keepdims=True)

    loads.wait(other_in_ready)
    act, slope = gelu_pair(contract(hidden_ref[...], other_in[...], 1, 0) + in_bias_of(biases_ref))
    act = act.astype(LOW)
    act_ref[...] = act
    loads.wait(other_down_ready)
    pre_two = base_ref[...] + contract(act, other_down[...], 1, 0)
    normed, scale = normalize(pre_two)
    output_ref[...] = (normed * gain_two + shift_two).astype(LOW)
    cot = cot_ref[...].astype(WIDE)
    grad_pre_two = normalize_back(cot, normed, scale, gain_two)
    count(sums_ref, 4, cot * normed)
    count(sums_ref, 5, cot)
    count(sums_ref, 3, grad_pre_two)
    branch_grad = grad_pre_two.astype(LOW)
    branch_ref[...] = branch_grad
    grad = contract(branch_grad, other_down[...], 1, 1) * slope
    count(bias_sums_ref, 1, grad)
    grad = grad.astype(LOW)
    other_grad_ref[...] = grad
    grad_hidden = grad_pre_two + contract(grad, other_in[...], 1, 1)
    loads.wait(own_down_ready)
    grad = contract(branch_grad, own_down[...], 1, 1) * slope_ref[...].astype(WIDE)
    count(bias_sums_ref, 0, grad)
    grad = grad.astype(LOW)
    own_grad_ref[...] = grad
    loads.wait(own_in_ready)
    grad_hidden += contract(grad, own_in[...], 1, 1)
    normed = normed_ref[...].astype(WIDE)
    grad_pre_one = normalize_back(grad_hidden, normed, scale_ref[...], gain_one)
    count(sums_ref, 1, grad_hidden * normed)
    count(sums_ref, 2, grad_hidden)
    count(sums_ref, 0, grad_pre_one)
    attended = grad_pre_one.astype(LOW)
    attended_ref[...] = attended
    loads.wait(out_ready)
    own_context_ref[...] = contract(attended, own_out[...], 1, 1).astype(LOW)
    other_context_ref[...] = contract(attended, other_out[...], 1, 1).astype(LOW)


def second_half(bits, hidden_low, base, cot, slope, normed, scale, vectors, biases, w_out, w_in, w_down, out_pieces, pieces):
    rows, width = hidden_low.shape
    local, hidden = w_out.shape[0], w_in.shape[1]
    tile = 256

    def row_block(columns):
        return pl.BlockSpec((tile, columns), lambda i, s: (i, 0))

    def whole(columns, count=1):
        return pl.BlockSpec((count, columns), lambda i, s: (0, 0))

    def low(columns):
        return jax.ShapeDtypeStruct((rows, columns), LOW)

    return pl.pallas_call(
        second_kernel,
        grid_spec=pltpu.PrefetchScalarGridSpec(
            num_scalar_prefetch=1,
            grid=(rows // tile,),
            in_specs=[
                row_block(width),
                row_block(width),
                row_block(width),
                row_block(hidden),
                row_block(width),
                row_block(1),
            ]
            + [pl.BlockSpec(array.shape, lambda i, s: (0, 0)) for array in (vectors, biases)]
            + [ANYWHERE] * (3 + len(out_pieces) + len(pieces)),
            out_specs=[
                row_block(width),
                row_block(width),
                row_block(hidden),
                row_block(hidden),
                row_block(hidden),
                row_block(width),
                row_block(local),
                row_block(local),
                whole(width, 8),
                whole(hidden, 8),
            ],
            scratch_shapes=[
                pltpu.VMEM((local, width), LOW),
                pltpu.VMEM((local, width), LOW),
                pltpu.VMEM((width, hidden), LOW),
                pltpu.VMEM((width, hidden), LOW),
                pltpu.VMEM((hidden, width), LOW),
                pltpu.VMEM((hidden, width), LOW),
                pltpu.SemaphoreType.DMA((23,)),
            ],
        ),
        out_shape=[
            low(width),
            low(width),
            low(hidden),
            low(hidden),
            low(hidden),
            low(width),
            low(local),
            low(local),
            jax.ShapeDtypeStruct((8, width), WIDE),
            jax.ShapeDtypeStruct((8, hidden), WIDE),
        ],
        cost_estimate=small_cost(),
        name="second_half",
    )(bits, hidden_low, base, cot, slope, normed, scale, vectors, biases, w_out, w_in, w_down, *out_pieces, *pieces)


def down_kernel(bits_ref, act_ref, grad_ref, sent_ref, kept_ref):
    z = bits_ref[2]
    result = contract(act_ref[...], grad_ref[...], 0, 0)
    rows = result.shape[0] // 2

    def put(out_ref):
        for part in range(2):
            out_ref[0, part ^ z] = result[part * rows : (part + 1) * rows].astype(LOW)

    @pl.when(pl.program_id(0) < 2)
    def _():
        put(sent_ref)

    @pl.when(pl.program_id(0) >= 2)
    def _():
        put(kept_ref)


def down_pieces(bits, activated, grad):
    rows, hidden = activated.shape
    width = grad.shape[1]
    piece = (1, 2, hidden // 8, width)
    return pl.pallas_call(
        down_kernel,
        grid_spec=pltpu.PrefetchScalarGridSpec(
            num_scalar_prefetch=1,
            grid=(4,),
            in_specs=[
                pl.BlockSpec(
                    (rows, hidden // 4), lambda i, s: (0, (s[0] ^ (1 - i // 2)) * 2 + ((i % 2) ^ s[1]))
                ),
                pl.BlockSpec((rows, width), lambda i, s: (0, 0)),
            ],
            out_specs=[
                pl.BlockSpec(piece, lambda i, s: (jnp.minimum(i, 1), 0, 0, 0)),
                pl.BlockSpec(piece, lambda i, s: (jnp.maximum(i - 2, 0), 0, 0, 0)),
            ],
        ),
        out_shape=[jax.ShapeDtypeStruct((2,) + piece[1:], LOW)] * 2,
        cost_estimate=small_cost(),
        name="down_pieces",
    )(bits, activated, grad)


def in_kernel(bits_ref, hidden_ref, grad_ref, sent_ref, kept_ref):
    x, z = bits_ref[1], bits_ref[2]
    result = contract(hidden_ref[...], grad_ref[...], 0, 0)
    rows, columns = result.shape[0] // 2, result.shape[1] // 2

    def put(out_ref):
        for side in range(2):
            for part in range(2):
                out_ref[side ^ x, part ^ z] = result[
                    part * rows : (part + 1) * rows, side * columns : (side + 1) * columns
                ].astype(LOW)

    @pl.when(pl.program_id(0) == 0)
    def _():
        put(sent_ref)

    @pl.when(pl.program_id(0) == 1)
    def _():
        put(kept_ref)


def in_pieces(bits, hidden_low, grad):
    rows, width = hidden_low.shape
    hidden = grad.shape[1]
    piece = (2, 2, width // 2, hidden // 4)
    return pl.pallas_call(
        in_kernel,
        grid_spec=pltpu.PrefetchScalarGridSpec(
            num_scalar_prefetch=1,
            grid=(2,),
            in_specs=[
                pl.BlockSpec((rows, width), lambda i, s: (0, 0)),
                pl.BlockSpec((rows, hidden // 2), lambda i, s: (0, s[0] ^ (1 - i))),
            ],
            out_specs=[pl.BlockSpec(piece, lambda i, s: (0, 0, 0, 0))] * 2,
        ),
        out_shape=[jax.ShapeDtypeStruct(piece, LOW)] * 2,
        cost_estimate=small_cost(),
        name="in_pieces",
    )(bits, hidden_low, grad)


def heads_kernel(bits_ref, x_ref, grads_ref, context_ref, attended_ref, sent_ref, kept_ref, scratch):
    core = bits_ref[0]
    mine = bits_ref[1] * 2 + bits_ref[2]
    extent, local = scratch.shape[1:]

    @pl.when(pl.program_id(0) < 3)
    def _():
        result = contract(x_ref[...], grads_ref[0], 0, 0)
        for part in range(8):
            scratch[part] = result[part * extent : (part + 1) * extent]

    @pl.when(pl.program_id(0) == 3)
    def _():
        result = contract(context_ref[...], attended_ref[...], 0, 0)
        for part in range(8):
            rows, side = part % 4, part // 4
            scratch[part] = result[rows * extent : (rows + 1) * extent, side * local : (side + 1) * local]

    for part in range(4):
        sent_ref[part ^ mine, 0] = scratch[(1 - core) * 4 + part].astype(LOW)
        kept_ref[part ^ mine, 0] = scratch[core * 4 + part].astype(LOW)


def heads_pieces(bits, tokens, grads, context, attended):
    rows, local = context.shape
    width = tokens.shape[1]
    return pl.pallas_call(
        heads_kernel,
        grid_spec=pltpu.PrefetchScalarGridSpec(
            num_scalar_prefetch=1,
            grid=(4,),
            in_specs=[
                pl.BlockSpec((rows, width), lambda j, s: (s[3], 0)),
                pl.BlockSpec((1, rows, local), lambda j, s: (jnp.minimum(j, 2), 0, 0)),
                pl.BlockSpec((rows, local), lambda j, s: (0, 0)),
                pl.BlockSpec((rows, width), lambda j, s: (0, 0)),
            ],
            out_specs=[pl.BlockSpec((4, 1, width // 8, local), lambda j, s: (0, j, 0, 0))] * 2,
            scratch_shapes=[pltpu.VMEM((8, width // 8, local), WIDE)],
        ),
        out_shape=[jax.ShapeDtypeStruct((4, 4, width // 8, local), LOW)] * 2,
        cost_estimate=small_cost(),
        name="heads_pieces",
    )(bits, tokens, grads, context, attended)


def add(*arrays):
    total = arrays[0].astype(WIDE)
    for array in arrays[1:]:
        total = total + array.astype(WIDE)
    return total.astype(LOW)


class Chain:
    AXES = {"x": 1, "z": 2}

    def __init__(self, order, size):
        self.order, self.size = order, size
        self.terms = {"own": [], "other": []}

    def begin(self, side, sent, kept):
        for array in (kept, swap(sent, 0, self.size)):
            self.terms[side].append((array, (), ("x", "z")))

    def summed(self, terms):
        def cut(*arrays):
            parts = []
            for array, (_, picks, _) in zip(arrays, terms):
                for axis, index in picks:
                    array = lax.index_in_dim(array, index, axis, False)
                parts.append(array)
            return add(*parts)

        return self.order.run(cut, *[array for array, _, _ in terms])

    def halve(self, side, name):
        def pick(term, index):
            array, picks, axes = term
            if name not in axes:
                return term
            left = tuple(axis for axis in axes if axis != name)
            return array, picks + ((axes.index(name), index),), left

        terms = self.terms[side]
        there = [pick(term, 1) for term in terms if name in term[2]]
        arrived = swap(self.summed(there), self.AXES[name], self.size)
        self.terms[side] = [pick(term, 0) for term in terms] + [(arrived, (), there[0][2])]

    def cross(self):
        terms = self.terms["other"]
        self.terms["own"].append((across(self.summed(terms)), (), terms[0][2]))

    def total(self):
        self.kept = self.summed(self.terms["own"])

    def exchange(self, bit):
        self.terms["own"] = [(array, (), ()) for array in (self.kept, swap(self.kept, bit, self.size))]

    def spread(self):
        self.pieces = [self.kept] + [swap(self.kept, bit, self.size) for bit in (2, 1, 0)]

    def spread_on(self):
        kept, z, x, partner = self.pieces
        (z,) = self.order.sync(z)
        self.pieces = [kept, z, x, swap(z, 1, self.size), partner, swap(z, 0, self.size)]

    def finish(self):
        kept, z, x, xz, partner, partner_z = self.pieces
        x, xz = self.order.sync(x, xz)
        return [kept, z, x, xz, partner, partner_z, swap(x, 0, self.size), swap(xz, 0, self.size)]


def widen(bits, pieces, shapes, places):
    def kernel(bits_ref, *refs):
        sources, outs, (low, wide, semaphores) = refs[:8], refs[8:-3], refs[-3:]
        rank = bits_ref[0] * 4 + bits_ref[1] * 2 + bits_ref[2]
        loads = [pltpu.make_async_copy(sources[r], low.at[r], semaphores.at[r]) for r in range(8)]
        for load in loads:
            load.start()
        stores = []
        for r, load in enumerate(loads):
            load.wait()
            wide[r] = low[r].astype(WIDE)
            q = r ^ rank
            for part, target in places(q // 4, (q // 2) % 2, q % 2, wide.at[r], outs):
                stores.append(pltpu.make_async_copy(part, target, semaphores.at[8 + len(stores)]))
                stores[-1].start()
        for store in stores:
            store.wait()

    piece = pieces[0].shape
    return pl.pallas_call(
        kernel,
        grid_spec=pltpu.PrefetchScalarGridSpec(
            num_scalar_prefetch=1,
            grid=(1,),
            in_specs=[ANYWHERE] * 8,
            out_specs=[ANYWHERE] * len(shapes),
            scratch_shapes=[
                pltpu.VMEM((8,) + piece, LOW),
                pltpu.VMEM((8,) + piece, WIDE),
                pltpu.SemaphoreType.DMA((8 + 8 * len(shapes),)),
            ],
        ),
        out_shape=[jax.ShapeDtypeStruct(shape, WIDE) for shape in shapes],
        cost_estimate=small_cost(),
        name="widen",
    )(bits, *pieces)


def stretch(index, extent, unit):
    return pl.ds(pl.multiple_of(index * extent, unit), extent)


def down_places(core, x, z, piece, outs):
    return [(piece, outs[0].at[stretch(core * 4 + x * 2 + z, piece.shape[0], 8)])]


def in_places(core, x, z, piece, outs):
    rows, columns = piece.shape
    return [(piece, outs[0].at[stretch(z, rows, 8), stretch(core * 2 + x, columns, 128)])]


def heads_places(core, x, z, piece, outs):
    _, rows, columns = piece.shape
    return [
        (piece.at[:3], outs[0].at[:, stretch(core * 4 + x * 2 + z, rows, 8)]),
        (piece.at[3], outs[1].at[stretch(x * 2 + z, rows, 8), stretch(core, columns, 128)]),
    ]


def body(
    tokens,
    lengths,
    w_qkv,
    q_bias,
    v_bias,
    w_out,
    out_bias,
    gain_one,
    shift_one,
    w_in,
    in_bias,
    w_down,
    down_bias,
    gain_two,
    shift_two,
    cotangent,
):
    width, hidden = w_in.shape
    local = w_qkv.shape[2]
    sequences = lengths.shape[0] // 2
    size = lax.axis_size("dp")
    extra = range(3, size.bit_length() - 1)
    dp = lax.axis_index("dp")
    bits = jnp.stack([dp & 1, (dp >> 1) & 1, (dp >> 2) & 1, lax.axis_index("tensor")]).astype(jnp.int32)

    qkv_own = jnp.transpose(w_qkv, (1, 0, 2))
    attention_piece, forward_piece = pack(bits, qkv_own, w_out, w_in, w_down)
    order = Order(attention_piece)
    attention_fetch = Fetch(order, attention_piece, size)
    biases = order.run(
        lambda *vectors: jnp.concatenate([v.reshape(-1, local) for v in vectors]), q_bias, v_bias, in_bias
    )
    vectors = order.run(
        lambda *vectors: jnp.stack(vectors), out_bias, gain_one, shift_one, down_bias, gain_two, shift_two
    )
    biases_other = across(biases)
    (forward_piece,) = order.sync(forward_piece)
    forward_fetch = Fetch(order, forward_piece, size)

    q_own, k_own, v_own = order.run(lambda x: project(bits, x, biases, [qkv_own]), tokens)
    attention_fetch.pass_on()
    context_own, probs_own = order.run(
        lambda *qkv: attend(bits, lengths, *qkv), q_own, k_own, v_own
    )
    attention_pieces = attention_fetch.finish()
    q_other, k_other, v_other = order.run(
        lambda biases, *parts: project(bits, tokens, biases, parts), biases_other, *attention_pieces
    )
    forward_fetch.pass_on()
    context_other, probs_other = order.run(
        lambda *qkv: attend(bits, lengths, *qkv), q_other, k_other, v_other
    )
    hidden_low, normed_one, scale_one, base, act_own, slope_own = order.run(
        lambda own, other: first_half(
            bits, own, other, tokens, vectors, biases, w_out, w_in, w_down, attention_pieces
        ),
        context_own,
        context_other,
    )
    forward_pieces = forward_fetch.finish()
    (
        output,
        branch_grad,
        act_other,
        grad_own,
        grad_other,
        attended_grad,
        context_grad_own,
        context_grad_other,
        sums,
        bias_sums,
    ) = order.run(
        lambda hidden_low, *pieces: second_half(
            bits,
            hidden_low,
            base,
            cotangent,
            slope_own,
            normed_one,
            scale_one,
            vectors,
            biases_other,
            w_out,
            w_in,
            w_down,
            attention_pieces,
            pieces,
        ),
        hidden_low,
        *forward_pieces,
    )

    down, entry, heads = Chain(order, size), Chain(order, size), Chain(order, size)

    def down_grad(act):
        return order.run(lambda act: down_pieces(bits, act, branch_grad), act)

    def in_grad(grad):
        return order.run(lambda grad: in_pieces(bits, hidden_low, grad), grad)

    def heads_back(q, k, v, context, context_grad, probs):
        return order.run(
            lambda *args: attend_back(*args, sequences), q, k, v, context, context_grad, probs
        )

    def heads_grad(grads, context):
        pieces = order.run(
            lambda grads: heads_pieces(bits, tokens, grads, context, attended_grad), grads
        )
        return [piece.reshape(2, 2, *piece.shape[1:]) for piece in pieces]

    def head_sums(grads):
        return [jnp.sum(grads[0].astype(WIDE), axis=0), jnp.sum(grads[2].astype(WIDE), axis=0)]

    down.begin("other", *down_grad(act_other))
    entry.begin("other", *in_grad(grad_other))
    down.cross()
    entry.begin("own", *in_grad(grad_own))
    entry.halve("other", "x")
    down.begin("own", *down_grad(act_own))
    project_other = heads_back(
        q_other, k_other, v_other, context_other, context_grad_other, probs_other
    )
    entry.halve("own", "x")
    entry.cross()
    down.halve("own", "x")
    heads.begin("other", *heads_grad(project_other, context_other))
    other_sums = order.run(
        lambda grads, sums: jnp.concatenate([sums[:6].reshape(-1), bias_sums[1]] + head_sums(grads)),
        project_other,
        sums,
    )
    heads.cross()
    project_own = heads_back(q_own, k_own, v_own, context_own, context_grad_own, probs_own)
    entry.halve("own", "z")
    down.halve("own", "z")
    heads.begin("own", *heads_grad(project_own, context_own))
    arrived = across(other_sums)
    entry.total()
    if extra:
        entry.exchange(extra[0])
    down.total()
    if extra:
        down.exchange(extra[0])
    input_grad = order.run(
        lambda *grads: project_back(bits, *grads, attended_grad, qkv_own, attention_pieces),
        project_own,
        project_other,
    )
    totals = order.run(
        lambda grads, sums, arrived: jnp.concatenate(
            [sums[:6].reshape(-1), bias_sums[0]] + head_sums(grads)
        )
        + arrived,
        project_own,
        sums,
        arrived,
    )
    arrived = swap(totals, 0, size)
    heads.halve("own", "x")
    totals = order.run(jnp.add, totals, arrived)
    arrived = swap(totals, 1, size)
    for bit in extra:
        entry.total()
        if bit + 1 in extra:
            entry.exchange(bit + 1)
        down.total()
        if bit + 1 in extra:
            down.exchange(bit + 1)
    entry.spread()
    down.spread()
    totals = order.run(jnp.add, totals, arrived)
    arrived = swap(totals, 2, size)
    heads.halve("own", "z")
    entry.spread_on()
    down.spread_on()
    totals = order.run(jnp.add, totals, arrived)
    heads.total()
    entry_pieces = entry.finish()
    down_pieces_all = down.finish()
    for bit in extra:
        heads.exchange(bit)
        arrived = swap(totals, bit, size)
        if bit == extra[0]:
            (grad_w_in,) = order.run(
                lambda *pieces: widen(bits, pieces, [(width, hidden)], in_places), *entry_pieces
            )
        totals = order.run(jnp.add, totals, arrived)
        heads.total()
    heads.spread()
    (grad_w_down,) = order.run(
        lambda *pieces: widen(bits, pieces, [(hidden, width)], down_places), *down_pieces_all
    )
    heads.spread_on()
    count = 6 * width
    shared = totals[:count].reshape(6, width)
    grad_in_bias = totals[count : count + hidden]
    head_biases = totals[count + hidden :]
    grad_qkv, grad_w_out = order.run(
        lambda *pieces: widen(bits, pieces, [(3, width, local), (local, width)], heads_places),
        *heads.finish(),
    )

    return (
        output,
        input_grad,
        jnp.transpose(grad_qkv, (1, 0, 2)),
        head_biases[:local],
        head_biases[local:],
        grad_w_out,
        shared[0],
        shared[1],
        shared[2],
        grad_w_in,
        grad_in_bias,
        grad_w_down,
        shared[3],
        shared[4],
        shared[5],
    )


def solution(mesh):
    placed = (
        P("dp", None),
        P("dp"),
        P(None, None, "tensor"),
        P("tensor"),
        P("tensor"),
        P("tensor", None),
        P(),
        P(),
        P(),
        P(None, "tensor"),
        P("tensor"),
        P("tensor", None),
        P(),
        P(),
        P(),
        P(("dp", "tensor"), None),
    )
    return jax.shard_map(
        body,
        mesh=mesh,
        in_specs=placed,
        out_specs=(
            P(("dp", "tensor"), None),
            P(("dp", "tensor"), None),
            P(None, None, "tensor"),
            P("tensor"),
            P("tensor"),
            P("tensor", None),
            P(),
            P(),
            P(),
            P(None, "tensor"),
            P("tensor"),
            P("tensor", None),
            P(),
            P(),
            P(),
        ),
        check_vma=False,
    )
```

```python
import jax
import jax.numpy as jnp
from jax import lax
from jax.experimental import pallas as pl
from jax.experimental.pallas import tpu as pltpu
from jax.sharding import PartitionSpec as P

HEAD_DIM = 64
EPSILON = 1e-06
MASKED = -1000000000.0
LOW = jnp.bfloat16
WIDE = jnp.float32
RSQRT2PI = 0.3989422804014327


def contract(a, b, dim_a, dim_b):
    return lax.dot_general(
        a, b, (((dim_a,), (dim_b,)), ((), ())), preferred_element_type=WIDE
    )


def swap(array, bit, size):
    return lax.ppermute(array, "dp", [(i, i ^ (1 << bit)) for i in range(size)])


def across(array):
    return lax.ppermute(array, "tensor", [(0, 1), (1, 0)])


ANYWHERE = pl.BlockSpec(memory_space=pl.ANY)


def cost(flops):
    return pl.CostEstimate(flops=flops, bytes_accessed=10**5, transcendentals=0)


def attend_kernel(bits_ref, length_ref, q_ref, k_ref, v_ref, context_ref, probs_ref):
    length = length_ref[bits_ref[3] * pl.num_programs(0) + pl.program_id(0)]
    rows = q_ref.shape[0]
    lane = lax.broadcasted_iota(jnp.int32, (rows, 128), 1)
    slot = lax.broadcasted_iota(jnp.int32, (rows, 128), 0)
    masked = jnp.where(slot < length, 0.0, MASKED).astype(LOW)
    q, k, v = q_ref[...], k_ref[...], v_ref[...]
    zero, one = jnp.zeros_like(q), jnp.ones_like(q)
    contexts = []
    for head in range(2):
        mine = (lane >= 64) if head else (lane < 64)
        mark = lane == (0 if head else 64)
        k_head = jnp.where(mine, k, jnp.where(mark, masked, zero))
        q_head = jnp.where(mine, q, jnp.where(mark, one, zero))
        scores = contract(k_head, q_head, 1, 1)
        top = jnp.max(scores, axis=0, keepdims=True)
        exponent = jnp.exp(scores - top)
        total = jnp.sum(exponent, axis=0, keepdims=True)
        probs = (exponent * (1.0 / total)).astype(LOW)
        probs_ref[head] = probs
        contexts.append(contract(probs, v, 0, 0))
    context_ref[...] = jnp.where(lane < 64, contexts[0], contexts[1]).astype(LOW)


def attend(bits, lengths, q, k, v):
    rows, width = q.shape
    sequences = lengths.shape[0] // 2
    length, pairs = rows // sequences, width // 128
    block = pl.BlockSpec((length, 128), lambda s, h, *_: (s, h))
    return pl.pallas_call(
        attend_kernel,
        grid_spec=pltpu.PrefetchScalarGridSpec(
            num_scalar_prefetch=2,
            grid=(sequences, pairs),
            in_specs=[block] * 3,
            out_specs=[
                block,
                pl.BlockSpec((2, length, length), lambda s, h, *_: (s * pairs + h, 0, 0)),
            ],
        ),
        out_shape=[
            jax.ShapeDtypeStruct((rows, width), LOW),
            jax.ShapeDtypeStruct((sequences * pairs * 2, length, length), LOW),
        ],
        cost_estimate=cost(10**6),
        name="attend",
    )(bits, lengths, q, k, v)


def attend_back_kernel(q_ref, k_ref, v_ref, context_ref, grad_ref, probs_ref, out_ref):
    rows = q_ref.shape[0]
    lane = lax.broadcasted_iota(jnp.int32, (rows, 128), 1)
    q, k, v, grad = q_ref[...], k_ref[...], v_ref[...], grad_ref[...]
    inner = pltpu.roll(grad.astype(WIDE) * context_ref[...].astype(WIDE), 64, 1).astype(LOW)
    zero, minus = jnp.zeros_like(q), -jnp.ones_like(q)
    grad_q = grad_k = grad_v = 0.0
    for head in range(2):
        mine = (lane >= 64) if head else (lane < 64)
        centred = contract(jnp.where(mine, v, minus), jnp.where(mine, grad, inner), 1, 1)
        probs = probs_ref[head]
        grad_scores = (probs.astype(WIDE) * centred).astype(LOW)
        grad_v += contract(probs, jnp.where(mine, grad, zero), 1, 0)
        grad_k += contract(grad_scores, jnp.where(mine, q, zero), 1, 0)
        grad_q += contract(grad_scores, jnp.where(mine, k, zero), 0, 0)
    out_ref[0] = (grad_q * HEAD_DIM**-0.5).astype(LOW)
    out_ref[1] = grad_k.astype(LOW)
    out_ref[2] = grad_v.astype(LOW)


def attend_back(q, k, v, context, grad, probs, sequences):
    rows, width = q.shape
    length, pairs = rows // sequences, width // 128
    block = pl.BlockSpec((length, 128), lambda s, h: (s, h))
    return pl.pallas_call(
        attend_back_kernel,
        grid=(sequences, pairs),
        in_specs=[block] * 5
        + [pl.BlockSpec((2, length, length), lambda s, h: (s * pairs + h, 0, 0))],
        out_specs=pl.BlockSpec((3, length, 128), lambda s, h: (0, s, h)),
        out_shape=jax.ShapeDtypeStruct((3, rows, width), LOW),
        cost_estimate=cost(2 * 10**10),
        name="attend_back",
    )(q, k, v, context, grad, probs)


def pack_kernel(bits_ref, qkv_ref, out_ref, in_ref, down_ref, attention_ref, forward_ref):
    attention_ref[:3] = qkv_ref[...]
    for target, source in ((attention_ref.at[3], out_ref), (forward_ref, in_ref)):
        rows, width = source.shape[0], source.shape[1] // 2
        for side in range(2):
            target[side * rows : (side + 1) * rows] = source[:, side * width : (side + 1) * width]
    rows = down_ref.shape[0]
    forward_ref[rows:] = down_ref[...]


def pack(bits, w_qkv, w_out, w_in, w_down):
    quarters = [(3, w_qkv.shape[1] // 4, w_qkv.shape[2])]
    quarters += [(w.shape[0] // 4, w.shape[1]) for w in (w_out, w_in, w_down)]
    _, rows, local = quarters[0]
    attention, forward = (4, rows, local), (2 * quarters[3][0], quarters[3][1])

    def place(*index):
        return lambda i, s: tuple(s[0] * 2 + s[1] if k else 0 for k in index)

    return pl.pallas_call(
        pack_kernel,
        grid_spec=pltpu.PrefetchScalarGridSpec(
            num_scalar_prefetch=1,
            grid=(1,),
            in_specs=[pl.BlockSpec(quarters[0], place(0, 1, 0))]
            + [pl.BlockSpec(quarter, place(1, 0)) for quarter in quarters[1:]],
            out_specs=[pl.BlockSpec(attention, place(0, 0, 0)), pl.BlockSpec(forward, place(0, 0))],
        ),
        out_shape=[jax.ShapeDtypeStruct(attention, LOW), jax.ShapeDtypeStruct(forward, LOW)],
        cost_estimate=cost(10**6),
        name="pack",
    )(bits, w_qkv, w_out, w_in, w_down)


class Order:
    def __init__(self, first):
        self.last = first

    def sync(self, *arrays):
        arrays, self.last = lax.optimization_barrier((arrays, self.last))
        return arrays

    def run(self, step, *arrays):
        arrays = self.sync(*arrays)
        result = step(*arrays)
        self.last = result[0] if isinstance(result, (list, tuple)) else result
        return result


class Fetch:
    def __init__(self, order, piece, size):
        self.order, self.size = order, size
        self.here = across(piece)

    def pass_on(self, *others):
        self.here, *others = self.order.sync(self.here, *others)
        self.x = swap(self.here, 1, self.size)
        self.partner = swap(self.here, 0, self.size)
        return others

    def finish(self):
        (self.x,) = self.order.sync(self.x)
        return [self.here, self.x, self.partner, swap(self.x, 0, self.size)]


def rank_of(bits_ref):
    return bits_ref[0] * 2 + bits_ref[1]


class Loads:
    def __init__(self, semaphores):
        self.semaphores, self.count, self.groups = semaphores, 0, []

    def group(self, pairs):
        copies = []
        for source, target in pairs:
            copies.append(pltpu.make_async_copy(source, target, self.semaphores.at[self.count]))
            self.count += 1
        self.groups.append(copies)
        return len(self.groups) - 1

    def start(self):
        @pl.when(pl.program_id(0) == 0)
        def _():
            for copies in self.groups:
                for copy in copies:
                    copy.start()

    def wait(self, group):
        @pl.when(pl.program_id(0) == 0)
        def _():
            for copy in self.groups[group]:
                copy.wait()


def qkv_parts(parts, target, rank):
    extent = target.shape[1] // 4
    return [
        (part.at[:3], target.at[:, pl.ds(pl.multiple_of((r ^ rank) * extent, 16), extent)])
        for r, part in enumerate(parts)
    ]


def out_parts(parts, target, rank):
    extent, width = target.shape[0] // 4, target.shape[1] // 2
    return [
        (
            part.at[3, pl.ds(side * extent, extent)],
            target.at[pl.ds(pl.multiple_of((r ^ rank) * extent, 16), extent), pl.ds(side * width, width)],
        )
        for r, part in enumerate(parts)
        for side in range(2)
    ]


def in_parts(parts, target, rank):
    extent, width = target.shape[0] // 4, target.shape[1] // 2
    return [
        (
            part.at[pl.ds(side * extent, extent)],
            target.at[pl.ds(pl.multiple_of((r ^ rank) * extent, 16), extent), pl.ds(side * width, width)],
        )
        for r, part in enumerate(parts)
        for side in range(2)
    ]


def down_parts(parts, target, rank):
    extent = target.shape[0] // 4
    return [
        (part.at[pl.ds(extent, extent)], target.at[pl.ds(pl.multiple_of((r ^ rank) * extent, 16), extent)])
        for r, part in enumerate(parts)
    ]


def project_kernel(bits_ref, x_ref, biases_ref, *refs):
    parts, (q_ref, k_ref, v_ref, weights, semaphores) = refs[:-5], refs[-5:]
    loads = Loads(semaphores)
    if len(parts) == 1:
        ready = loads.group([(parts[0], weights)])
    else:
        ready = loads.group(qkv_parts(parts, weights, rank_of(bits_ref)))
    loads.start()
    loads.wait(ready)
    x = x_ref[...]
    queries = (contract(x, weights[0], 1, 0) + biases_ref[0:1]).astype(LOW)
    q_ref[...] = queries * HEAD_DIM**-0.5
    k_ref[...] = contract(x, weights[1], 1, 0).astype(LOW)
    v_ref[...] = (contract(x, weights[2], 1, 0) + biases_ref[1:2]).astype(LOW)


def project(bits, tokens, biases, parts):
    rows, width = tokens.shape[0] // 2, tokens.shape[1]
    local = biases.shape[1]
    tile = 512
    steps = rows // tile
    return pl.pallas_call(
        project_kernel,
        grid_spec=pltpu.PrefetchScalarGridSpec(
            num_scalar_prefetch=1,
            grid=(steps,),
            in_specs=[
                pl.BlockSpec((tile, width), lambda i, s: (s[3] * steps + i, 0)),
                pl.BlockSpec(biases.shape, lambda i, s: (0, 0)),
            ]
            + [ANYWHERE] * len(parts),
            out_specs=[pl.BlockSpec((tile, local), lambda i, s: (i, 0))] * 3,
            scratch_shapes=[pltpu.VMEM((3, width, local), LOW), pltpu.SemaphoreType.DMA((4,))],
        ),
        out_shape=[jax.ShapeDtypeStruct((rows, local), LOW)] * 3,
        cost_estimate=cost(10**6),
        name="project",
    )(bits, tokens, biases, *parts)


def project_back_kernel(bits_ref, own_ref, other_ref, grad_ref, weights_ref, *refs):
    parts, (out_ref, own_weights, other_weights, semaphores) = refs[:-4], refs[-4:]
    loads = Loads(semaphores)
    own_ready = loads.group([(weights_ref, own_weights)])
    other_ready = loads.group(qkv_parts(parts, other_weights, rank_of(bits_ref)))
    loads.start()
    loads.wait(own_ready)
    total = grad_ref[...].astype(WIDE)
    for index in range(3):
        total += contract(own_ref[index], own_weights[index], 1, 1)
    loads.wait(other_ready)
    for index in range(3):
        total += contract(other_ref[index], other_weights[index], 1, 1)
    out_ref[...] = total.astype(LOW)


def project_back(bits, own, other, grad, weights, parts):
    rows, width = grad.shape
    local = own.shape[2]
    tile = 256
    block = pl.BlockSpec((3, tile, local), lambda i, s: (0, i, 0))
    row_block = pl.BlockSpec((tile, width), lambda i, s: (i, 0))
    return pl.pallas_call(
        project_back_kernel,
        grid_spec=pltpu.PrefetchScalarGridSpec(
            num_scalar_prefetch=1,
            grid=(rows // tile,),
            in_specs=[block, block, row_block] + [ANYWHERE] * (1 + len(parts)),
            out_specs=row_block,
            scratch_shapes=[pltpu.VMEM((3, width, local), LOW)] * 2 + [pltpu.SemaphoreType.DMA((5,))],
        ),
        out_shape=jax.ShapeDtypeStruct((rows, width), LOW),
        cost_estimate=cost(2 * 10**10),
        name="project_back",
    )(bits, own, other, grad, weights, *parts)


def normalize(values):
    average = jnp.mean(values, axis=-1, keepdims=True)
    centred = values - average
    scale = lax.rsqrt(jnp.mean(centred * centred, axis=-1, keepdims=True) + EPSILON)
    return centred * scale, scale


def normalize_back(grad, normed, scale, gain):
    grad_normed = grad * gain
    first = jnp.mean(grad_normed, axis=-1, keepdims=True)
    second = jnp.mean(grad_normed * normed, axis=-1, keepdims=True)
    return scale * (grad_normed - first - normed * second)


TAIL = (
    0.0356748104095459,
    -0.15720322728157043,
    0.20635373890399933,
    -0.053683843463659286,
    0.12856172025203705,
    0.09991346299648285,
    0.12075395882129669,
    0.11962930113077164,
)


def gelu_pair(values):
    t = 1.0 / (1.0 + 0.3 * jnp.abs(values))
    bell = jnp.exp(-0.5 * (values * values))
    series = TAIL[0]
    for coefficient in TAIL[1:]:
        series = series * t + coefficient
    tail = bell * (t * series)
    below = jnp.where(values < 0.0, tail, 1.0 - tail)
    return values * below, below + RSQRT2PI * (values * bell)


def in_bias_of(biases_ref):
    return jnp.concatenate([biases_ref[i : i + 1] for i in range(2, biases_ref.shape[0])], axis=1)


def first_kernel(
    bits_ref,
    own_context_ref,
    other_context_ref,
    x_ref,
    vectors_ref,
    biases_ref,
    w_out_ref,
    w_in_ref,
    w_down_ref,
    *refs,
):
    parts = refs[:4]
    hidden_ref, normed_ref, scale_ref, base_ref, act_ref, slope_ref = refs[4:10]
    own_out, other_out, w_in, w_down, semaphores = refs[10:]
    out_bias, gain, shift, down_bias = [vectors_ref[i : i + 1] for i in range(4)]
    loads = Loads(semaphores)
    out_ready = loads.group([(w_out_ref, own_out)] + out_parts(parts, other_out, rank_of(bits_ref)))
    in_ready = loads.group([(w_in_ref, w_in)])
    down_ready = loads.group([(w_down_ref, w_down)])
    loads.start()
    loads.wait(out_ready)
    pre_one = contract(own_context_ref[...], own_out[...], 1, 0)
    pre_one += contract(other_context_ref[...], other_out[...], 1, 0)
    pre_one += out_bias + x_ref[...].astype(WIDE)
    normed, scale = normalize(pre_one)
    hidden = normed * gain + shift
    hidden_low = hidden.astype(LOW)
    hidden_ref[...] = hidden_low
    normed_ref[...] = normed.astype(LOW)
    scale_ref[...] = scale
    loads.wait(in_ready)
    act, slope = gelu_pair(contract(hidden_low, w_in[...], 1, 0) + in_bias_of(biases_ref))
    act = act.astype(LOW)
    act_ref[...] = act
    slope_ref[...] = slope.astype(LOW)
    loads.wait(down_ready)
    base_ref[...] = hidden + down_bias + contract(act, w_down[...], 1, 0)


def first_half(bits, own_context, other_context, tokens, vectors, biases, w_out, w_in, w_down, parts):
    rows, local = own_context.shape
    width, hidden = w_in.shape
    tile = 256
    steps = rows // tile

    def row_block(columns):
        return pl.BlockSpec((tile, columns), lambda i, s: (i, 0))

    def whole(array):
        return pl.BlockSpec(array.shape, lambda i, s: (0, 0))

    return pl.pallas_call(
        first_kernel,
        grid_spec=pltpu.PrefetchScalarGridSpec(
            num_scalar_prefetch=1,
            grid=(rows // tile,),
            in_specs=[row_block(local), row_block(local)]
            + [pl.BlockSpec((tile, width), lambda i, s: (s[3] * steps + i, 0))]
            + [whole(vectors), whole(biases)]
            + [ANYWHERE] * (3 + len(parts)),
            out_specs=[
                row_block(width),
                row_block(width),
                row_block(1),
                row_block(width),
                row_block(hidden),
                row_block(hidden),
            ],
            scratch_shapes=[
                pltpu.VMEM((local, width), LOW),
                pltpu.VMEM((local, width), LOW),
                pltpu.VMEM((width, hidden), LOW),
                pltpu.VMEM((hidden, width), LOW),
                pltpu.SemaphoreType.DMA((11,)),
            ],
        ),
        out_shape=[
            jax.ShapeDtypeStruct((rows, width), LOW),
            jax.ShapeDtypeStruct((rows, width), LOW),
            jax.ShapeDtypeStruct((rows, 1), WIDE),
            jax.ShapeDtypeStruct((rows, width), WIDE),
            jax.ShapeDtypeStruct((rows, hidden), LOW),
            jax.ShapeDtypeStruct((rows, hidden), LOW),
        ],
        cost_estimate=cost(10**6),
        name="first_half",
    )(bits, own_context, other_context, tokens, vectors, biases, w_out, w_in, w_down, *parts)


def second_kernel(
    bits_ref,
    hidden_ref,
    base_ref,
    cot_ref,
    slope_ref,
    normed_ref,
    scale_ref,
    vectors_ref,
    biases_ref,
    w_out_ref,
    w_in_ref,
    w_down_ref,
    *refs,
):
    out_pieces, pieces = refs[:4], refs[4:8]
    output_ref, branch_ref, act_ref, own_grad_ref, other_grad_ref, attended_ref = refs[8:14]
    own_context_ref, other_context_ref, sums_ref, bias_sums_ref = refs[14:18]
    own_out, other_out, own_in, other_in, own_down, other_down, semaphores = refs[18:]
    gain_one, gain_two, shift_two = vectors_ref[1:2], vectors_ref[4:5], vectors_ref[5:6]
    rank = rank_of(bits_ref)
    loads = Loads(semaphores)
    other_in_ready = loads.group(in_parts(pieces, other_in, rank))
    other_down_ready = loads.group(down_parts(pieces, other_down, rank))
    own_down_ready = loads.group([(w_down_ref, own_down)])
    own_in_ready = loads.group([(w_in_ref, own_in)])
    out_ready = loads.group([(w_out_ref, own_out)] + out_parts(out_pieces, other_out, rank))
    loads.start()

    @pl.when(pl.program_id(0) == 0)
    def _():
        sums_ref[...] = jnp.zeros_like(sums_ref)
        bias_sums_ref[...] = jnp.zeros_like(bias_sums_ref)

    def count(ref, row, values):
        ref[row : row + 1] += jnp.sum(values, axis=0, keepdims=True)

    loads.wait(other_in_ready)
    act, slope = gelu_pair(contract(hidden_ref[...], other_in[...], 1, 0) + in_bias_of(biases_ref))
    act = act.astype(LOW)
    act_ref[...] = act
    loads.wait(other_down_ready)
    pre_two = base_ref[...] + contract(act, other_down[...], 1, 0)
    normed, scale = normalize(pre_two)
    output_ref[...] = (normed * gain_two + shift_two).astype(LOW)
    cot = cot_ref[...].astype(WIDE)
    grad_pre_two = normalize_back(cot, normed, scale, gain_two)
    count(sums_ref, 4, cot * normed)
    count(sums_ref, 5, cot)
    count(sums_ref, 3, grad_pre_two)
    branch_grad = grad_pre_two.astype(LOW)
    branch_ref[...] = branch_grad
    grad = contract(branch_grad, other_down[...], 1, 1) * slope
    count(bias_sums_ref, 1, grad)
    grad = grad.astype(LOW)
    other_grad_ref[...] = grad
    grad_hidden = grad_pre_two + contract(grad, other_in[...], 1, 1)
    loads.wait(own_down_ready)
    grad = contract(branch_grad, own_down[...], 1, 1) * slope_ref[...].astype(WIDE)
    count(bias_sums_ref, 0, grad)
    grad = grad.astype(LOW)
    own_grad_ref[...] = grad
    loads.wait(own_in_ready)
    grad_hidden += contract(grad, own_in[...], 1, 1)
    normed = normed_ref[...].astype(WIDE)
    grad_pre_one = normalize_back(grad_hidden, normed, scale_ref[...], gain_one)
    count(sums_ref, 1, grad_hidden * normed)
    count(sums_ref, 2, grad_hidden)
    count(sums_ref, 0, grad_pre_one)
    attended = grad_pre_one.astype(LOW)
    attended_ref[...] = attended
    loads.wait(out_ready)
    own_context_ref[...] = contract(attended, own_out[...], 1, 1).astype(LOW)
    other_context_ref[...] = contract(attended, other_out[...], 1, 1).astype(LOW)


def second_half(bits, hidden_low, base, cot, slope, normed, scale, vectors, biases, w_out, w_in, w_down, out_pieces, pieces):
    rows, width = hidden_low.shape
    local, hidden = w_out.shape[0], w_in.shape[1]
    tile = 256

    def row_block(columns):
        return pl.BlockSpec((tile, columns), lambda i, s: (i, 0))

    def whole(columns, count=1):
        return pl.BlockSpec((count, columns), lambda i, s: (0, 0))

    def low(columns):
        return jax.ShapeDtypeStruct((rows, columns), LOW)

    return pl.pallas_call(
        second_kernel,
        grid_spec=pltpu.PrefetchScalarGridSpec(
            num_scalar_prefetch=1,
            grid=(rows // tile,),
            in_specs=[
                row_block(width),
                row_block(width),
                row_block(width),
                row_block(hidden),
                row_block(width),
                row_block(1),
            ]
            + [pl.BlockSpec(array.shape, lambda i, s: (0, 0)) for array in (vectors, biases)]
            + [ANYWHERE] * (3 + len(out_pieces) + len(pieces)),
            out_specs=[
                row_block(width),
                row_block(width),
                row_block(hidden),
                row_block(hidden),
                row_block(hidden),
                row_block(width),
                row_block(local),
                row_block(local),
                whole(width, 8),
                whole(hidden, 8),
            ],
            scratch_shapes=[
                pltpu.VMEM((local, width), LOW),
                pltpu.VMEM((local, width), LOW),
                pltpu.VMEM((width, hidden), LOW),
                pltpu.VMEM((width, hidden), LOW),
                pltpu.VMEM((hidden, width), LOW),
                pltpu.VMEM((hidden, width), LOW),
                pltpu.SemaphoreType.DMA((23,)),
            ],
        ),
        out_shape=[
            low(width),
            low(width),
            low(hidden),
            low(hidden),
            low(hidden),
            low(width),
            low(local),
            low(local),
            jax.ShapeDtypeStruct((8, width), WIDE),
            jax.ShapeDtypeStruct((8, hidden), WIDE),
        ],
        cost_estimate=cost(10**6),
        name="second_half",
    )(bits, hidden_low, base, cot, slope, normed, scale, vectors, biases, w_out, w_in, w_down, *out_pieces, *pieces)


def down_kernel(bits_ref, act_ref, grad_ref, sent_ref, kept_ref):
    z = bits_ref[2]
    result = contract(act_ref[...], grad_ref[...], 0, 0)
    rows = result.shape[0] // 2

    def put(out_ref):
        for part in range(2):
            out_ref[0, part ^ z] = result[part * rows : (part + 1) * rows].astype(LOW)

    @pl.when(pl.program_id(0) < 2)
    def _():
        put(sent_ref)

    @pl.when(pl.program_id(0) >= 2)
    def _():
        put(kept_ref)


def down_pieces(bits, activated, grad):
    rows, hidden = activated.shape
    width = grad.shape[1]
    piece = (1, 2, hidden // 8, width)
    return pl.pallas_call(
        down_kernel,
        grid_spec=pltpu.PrefetchScalarGridSpec(
            num_scalar_prefetch=1,
            grid=(4,),
            in_specs=[
                pl.BlockSpec(
                    (rows, hidden // 4), lambda i, s: (0, (s[0] ^ (1 - i // 2)) * 2 + ((i % 2) ^ s[1]))
                ),
                pl.BlockSpec((rows, width), lambda i, s: (0, 0)),
            ],
            out_specs=[
                pl.BlockSpec(piece, lambda i, s: (jnp.minimum(i, 1), 0, 0, 0)),
                pl.BlockSpec(piece, lambda i, s: (jnp.maximum(i - 2, 0), 0, 0, 0)),
            ],
        ),
        out_shape=[jax.ShapeDtypeStruct((2,) + piece[1:], LOW)] * 2,
        cost_estimate=cost(2 * 10**10),
        name="down_pieces",
    )(bits, activated, grad)


def in_kernel(bits_ref, hidden_ref, grad_ref, sent_ref, kept_ref):
    x, z = bits_ref[1], bits_ref[2]
    result = contract(hidden_ref[...], grad_ref[...], 0, 0)
    rows, columns = result.shape[0] // 2, result.shape[1] // 2

    def put(out_ref):
        for side in range(2):
            for part in range(2):
                out_ref[side ^ x, part ^ z] = result[
                    part * rows : (part + 1) * rows, side * columns : (side + 1) * columns
                ].astype(LOW)

    @pl.when(pl.program_id(0) == 0)
    def _():
        put(sent_ref)

    @pl.when(pl.program_id(0) == 1)
    def _():
        put(kept_ref)


def in_pieces(bits, hidden_low, grad):
    rows, width = hidden_low.shape
    hidden = grad.shape[1]
    piece = (2, 2, width // 2, hidden // 4)
    return pl.pallas_call(
        in_kernel,
        grid_spec=pltpu.PrefetchScalarGridSpec(
            num_scalar_prefetch=1,
            grid=(2,),
            in_specs=[
                pl.BlockSpec((rows, width), lambda i, s: (0, 0)),
                pl.BlockSpec((rows, hidden // 2), lambda i, s: (0, s[0] ^ (1 - i))),
            ],
            out_specs=[pl.BlockSpec(piece, lambda i, s: (0, 0, 0, 0))] * 2,
        ),
        out_shape=[jax.ShapeDtypeStruct(piece, LOW)] * 2,
        cost_estimate=cost(2 * 10**10),
        name="in_pieces",
    )(bits, hidden_low, grad)


def heads_kernel(bits_ref, x_ref, grads_ref, context_ref, attended_ref, sent_ref, kept_ref, scratch):
    core = bits_ref[0]
    mine = bits_ref[1] * 2 + bits_ref[2]
    extent, local = scratch.shape[1:]

    @pl.when(pl.program_id(0) < 3)
    def _():
        result = contract(x_ref[...], grads_ref[0], 0, 0)
        for part in range(8):
            scratch[part] = result[part * extent : (part + 1) * extent]

    @pl.when(pl.program_id(0) == 3)
    def _():
        result = contract(context_ref[...], attended_ref[...], 0, 0)
        for part in range(8):
            rows, side = part % 4, part // 4
            scratch[part] = result[rows * extent : (rows + 1) * extent, side * local : (side + 1) * local]

    for part in range(4):
        sent_ref[part ^ mine, 0] = scratch[(1 - core) * 4 + part].astype(LOW)
        kept_ref[part ^ mine, 0] = scratch[core * 4 + part].astype(LOW)


def heads_pieces(bits, tokens, grads, context, attended):
    rows, local = context.shape
    width = tokens.shape[1]
    return pl.pallas_call(
        heads_kernel,
        grid_spec=pltpu.PrefetchScalarGridSpec(
            num_scalar_prefetch=1,
            grid=(4,),
            in_specs=[
                pl.BlockSpec((rows, width), lambda j, s: (s[3], 0)),
                pl.BlockSpec((1, rows, local), lambda j, s: (jnp.minimum(j, 2), 0, 0)),
                pl.BlockSpec((rows, local), lambda j, s: (0, 0)),
                pl.BlockSpec((rows, width), lambda j, s: (0, 0)),
            ],
            out_specs=[pl.BlockSpec((4, 1, width // 8, local), lambda j, s: (0, j, 0, 0))] * 2,
            scratch_shapes=[pltpu.VMEM((8, width // 8, local), WIDE)],
        ),
        out_shape=[jax.ShapeDtypeStruct((4, 4, width // 8, local), LOW)] * 2,
        cost_estimate=cost(2 * 10**10),
        name="heads_pieces",
    )(bits, tokens, grads, context, attended)


def add(*arrays):
    total = arrays[0].astype(WIDE)
    for array in arrays[1:]:
        total = total + array.astype(WIDE)
    return total.astype(LOW)


class Chain:
    AXES = {"x": 1, "z": 2}

    def __init__(self, order, size):
        self.order, self.size = order, size
        self.terms = {"own": [], "other": []}

    def begin(self, side, sent, kept):
        for array in (kept, swap(sent, 0, self.size)):
            self.terms[side].append((array, (), ("x", "z")))

    def summed(self, terms):
        def cut(*arrays):
            parts = []
            for array, (_, picks, _) in zip(arrays, terms):
                for axis, index in picks:
                    array = lax.index_in_dim(array, index, axis, False)
                parts.append(array)
            return add(*parts)

        return self.order.run(cut, *[array for array, _, _ in terms])

    def halve(self, side, name):
        def pick(term, index):
            array, picks, axes = term
            if name not in axes:
                return term
            left = tuple(axis for axis in axes if axis != name)
            return array, picks + ((axes.index(name), index),), left

        terms = self.terms[side]
        there = [pick(term, 1) for term in terms if name in term[2]]
        arrived = swap(self.summed(there), self.AXES[name], self.size)
        self.terms[side] = [pick(term, 0) for term in terms] + [(arrived, (), there[0][2])]

    def cross(self):
        terms = self.terms["other"]
        self.terms["own"].append((across(self.summed(terms)), (), terms[0][2]))

    def total(self):
        self.kept = self.summed(self.terms["own"])

    def exchange(self, bits):
        if bits:
            arrived = swap(self.kept, bits[0], self.size)
            self.terms["own"] = [(array, (), ()) for array in (self.kept, arrived)]

    def fold(self, bits):
        while bits:
            bits = bits[1:]
            self.total()
            self.exchange(bits)

    def spread(self):
        self.z, self.x = swap(self.kept, 2, self.size), swap(self.kept, 1, self.size)

    def spread_on(self):
        (self.z,) = self.order.sync(self.z)
        self.far = swap(self.z, 1, self.size)

    def finish(self):
        mine = self.order.run(lambda *p: jnp.stack(p), self.kept, self.z, self.x, self.far)
        return mine, swap(mine, 0, self.size)


def widen(bits, pieces, shapes, places):
    def kernel(bits_ref, *refs):
        outs, (low, wide, semaphores) = refs[2:-3], refs[-3:]
        sources = [refs[r // 4].at[r % 4] for r in range(8)]
        rank = bits_ref[0] * 4 + bits_ref[1] * 2 + bits_ref[2]
        loads = [pltpu.make_async_copy(sources[r], low.at[r], semaphores.at[r]) for r in range(8)]
        for load in loads:
            load.start()
        stores = []
        for r, load in enumerate(loads):
            load.wait()
            wide[r] = low[r].astype(WIDE)
            q = r ^ rank
            for part, target in places(q // 4, (q // 2) % 2, q % 2, wide.at[r], outs):
                stores.append(pltpu.make_async_copy(part, target, semaphores.at[8 + len(stores)]))
                stores[-1].start()
        for store in stores:
            store.wait()

    piece = pieces[0].shape[1:]
    return pl.pallas_call(
        kernel,
        grid_spec=pltpu.PrefetchScalarGridSpec(
            num_scalar_prefetch=1,
            grid=(1,),
            in_specs=[ANYWHERE] * 2,
            out_specs=[ANYWHERE] * len(shapes),
            scratch_shapes=[
                pltpu.VMEM((8,) + piece, LOW),
                pltpu.VMEM((8,) + piece, WIDE),
                pltpu.SemaphoreType.DMA((8 + 8 * len(shapes),)),
            ],
        ),
        out_shape=[jax.ShapeDtypeStruct(shape, WIDE) for shape in shapes],
        cost_estimate=cost(2 * 10**10),
        name="widen",
    )(bits, *pieces)


def stretch(index, extent, unit):
    return pl.ds(pl.multiple_of(index * extent, unit), extent)


def down_places(core, x, z, piece, outs):
    return [(piece, outs[0].at[stretch(core * 4 + x * 2 + z, piece.shape[0], 8)])]


def in_places(core, x, z, piece, outs):
    rows, columns = piece.shape
    return [(piece, outs[0].at[stretch(z, rows, 8), stretch(core * 2 + x, columns, 128)])]


def heads_places(core, x, z, piece, outs):
    _, rows, columns = piece.shape
    return [
        (piece.at[:3], outs[0].at[:, stretch(core * 4 + x * 2 + z, rows, 8)]),
        (piece.at[3], outs[1].at[stretch(x * 2 + z, rows, 8), stretch(core, columns, 128)]),
    ]


def body(
    tokens,
    lengths,
    w_qkv,
    q_bias,
    v_bias,
    w_out,
    out_bias,
    gain_one,
    shift_one,
    w_in,
    in_bias,
    w_down,
    down_bias,
    gain_two,
    shift_two,
    cotangent,
):
    width, hidden = w_in.shape
    local = w_qkv.shape[2]
    sequences = lengths.shape[0] // 2
    size = lax.axis_size("dp")
    extra = range(3, size.bit_length() - 1)
    dp = lax.axis_index("dp")
    bits = jnp.stack([dp & 1, (dp >> 1) & 1, (dp >> 2) & 1, lax.axis_index("tensor")]).astype(jnp.int32)

    qkv_own = jnp.transpose(w_qkv, (1, 0, 2))
    attention_piece, forward_piece = pack(bits, qkv_own, w_out, w_in, w_down)
    order = Order(attention_piece)
    biases = order.run(
        lambda *vectors: jnp.concatenate([v.reshape(-1, local) for v in vectors]), q_bias, v_bias, in_bias
    )
    attention_fetch = Fetch(order, attention_piece, size)
    vectors = order.run(
        lambda *vectors: jnp.stack(vectors), out_bias, gain_one, shift_one, down_bias, gain_two, shift_two
    )
    biases_other = across(biases)
    (forward_piece,) = order.sync(forward_piece)
    forward_fetch = Fetch(order, forward_piece, size)

    q_own, k_own, v_own = order.run(lambda x: project(bits, x, biases, [qkv_own]), tokens)
    (biases_other,) = attention_fetch.pass_on(biases_other)
    context_own, probs_own = order.run(
        lambda *qkv: attend(bits, lengths, *qkv), q_own, k_own, v_own
    )
    attention_pieces = attention_fetch.finish()
    q_other, k_other, v_other = order.run(
        lambda biases, *parts: project(bits, tokens, biases, parts), biases_other, *attention_pieces
    )
    forward_fetch.pass_on()
    context_other, probs_other = order.run(
        lambda *qkv: attend(bits, lengths, *qkv), q_other, k_other, v_other
    )
    hidden_low, normed_one, scale_one, base, act_own, slope_own = order.run(
        lambda own, other: first_half(
            bits, own, other, tokens, vectors, biases, w_out, w_in, w_down, attention_pieces
        ),
        context_own,
        context_other,
    )
    forward_pieces = forward_fetch.finish()
    (
        output,
        branch_grad,
        act_other,
        grad_own,
        grad_other,
        attended_grad,
        context_grad_own,
        context_grad_other,
        sums,
        bias_sums,
    ) = order.run(
        lambda hidden_low, *pieces: second_half(
            bits,
            hidden_low,
            base,
            cotangent,
            slope_own,
            normed_one,
            scale_one,
            vectors,
            biases_other,
            w_out,
            w_in,
            w_down,
            attention_pieces,
            pieces,
        ),
        hidden_low,
        *forward_pieces,
    )

    down, entry, heads = Chain(order, size), Chain(order, size), Chain(order, size)

    def down_grad(act):
        return order.run(lambda act: down_pieces(bits, act, branch_grad), act)

    def in_grad(grad):
        return order.run(lambda grad: in_pieces(bits, hidden_low, grad), grad)

    def heads_back(q, k, v, context, context_grad, probs):
        return order.run(
            lambda *args: attend_back(*args, sequences), q, k, v, context, context_grad, probs
        )

    def heads_grad(grads, context):
        pieces = order.run(
            lambda grads: heads_pieces(bits, tokens, grads, context, attended_grad), grads
        )
        return [piece.reshape(2, 2, *piece.shape[1:]) for piece in pieces]

    def head_sums(grads):
        return [jnp.sum(grads[0].astype(WIDE), axis=0), jnp.sum(grads[2].astype(WIDE), axis=0)]

    down.begin("other", *down_grad(act_other))
    entry.begin("other", *in_grad(grad_other))
    down.cross()
    entry.begin("own", *in_grad(grad_own))
    entry.halve("other", "x")
    down.begin("own", *down_grad(act_own))
    project_other = heads_back(
        q_other, k_other, v_other, context_other, context_grad_other, probs_other
    )
    entry.halve("own", "x")
    entry.cross()
    down.halve("own", "x")
    heads.begin("other", *heads_grad(project_other, context_other))
    other_sums = order.run(
        lambda grads, sums: jnp.concatenate([sums[:6].reshape(-1), bias_sums[1]] + head_sums(grads)),
        project_other,
        sums,
    )
    heads.cross()
    project_own = heads_back(q_own, k_own, v_own, context_own, context_grad_own, probs_own)
    entry.halve("own", "z")
    down.halve("own", "z")
    heads.begin("own", *heads_grad(project_own, context_own))
    entry.total()
    entry.exchange(extra)
    down.total()
    down.exchange(extra)
    heads.halve("own", "x")
    arrived = across(other_sums)
    input_grad = order.run(
        lambda *grads: project_back(bits, *grads, attended_grad, qkv_own, attention_pieces),
        project_own,
        project_other,
    )
    totals = order.run(
        lambda grads, sums, arrived: jnp.concatenate(
            [sums[:6].reshape(-1), bias_sums[0]] + head_sums(grads)
        )
        + arrived,
        project_own,
        sums,
        arrived,
    )
    heads.halve("own", "z")
    entry.fold(extra)
    entry.spread()
    arrived = swap(totals, 0, size)
    heads.total()
    heads.exchange(extra)
    down.fold(extra)
    down.spread()
    entry.spread_on()
    totals = order.run(jnp.add, totals, arrived)
    down.spread_on()
    arrived = swap(totals, 1, size)
    entry_pieces = entry.finish()
    (grad_w_in,) = order.run(
        lambda *pieces: widen(bits, pieces, [(width, hidden)], in_places), *entry_pieces
    )
    heads.fold(extra)
    totals = order.run(jnp.add, totals, arrived)
    heads.spread()
    arrived = swap(totals, 2, size)
    (grad_w_down,) = order.run(
        lambda *pieces: widen(bits, pieces, [(hidden, width)], down_places), *down.finish()
    )
    totals = order.run(jnp.add, totals, arrived)
    heads.spread_on()
    for bit in extra:
        arrived = swap(totals, bit, size)
        totals = order.run(jnp.add, totals, arrived)
    count = 6 * width
    shared = totals[:count].reshape(6, width)
    grad_in_bias = totals[count : count + hidden]
    head_biases = totals[count + hidden :]
    grad_qkv, grad_w_out = order.run(
        lambda *pieces: widen(bits, pieces, [(3, width, local), (local, width)], heads_places),
        *heads.finish(),
    )

    return (
        output,
        input_grad,
        jnp.transpose(grad_qkv, (1, 0, 2)),
        head_biases[:local],
        head_biases[local:],
        grad_w_out,
        shared[0],
        shared[1],
        shared[2],
        grad_w_in,
        grad_in_bias,
        grad_w_down,
        shared[3],
        shared[4],
        shared[5],
    )


def solution(mesh):
    placed = (
        P("dp", None),
        P("dp"),
        P(None, None, "tensor"),
        P("tensor"),
        P("tensor"),
        P("tensor", None),
        P(),
        P(),
        P(),
        P(None, "tensor"),
        P("tensor"),
        P("tensor", None),
        P(),
        P(),
        P(),
        P(("dp", "tensor"), None),
    )
    return jax.shard_map(
        body,
        mesh=mesh,
        in_specs=placed,
        out_specs=(
            P(("dp", "tensor"), None),
            P(("dp", "tensor"), None),
            P(None, None, "tensor"),
            P("tensor"),
            P("tensor"),
            P("tensor", None),
            P(),
            P(),
            P(),
            P(None, "tensor"),
            P("tensor"),
            P("tensor", None),
            P(),
            P(),
            P(),
        ),
        check_vma=False,
    )
```
